256 devices in a mesh: dom: 32 (over y_hi, z, core), hid: 8 (over y_lo, x).
Axes of the slice: x: 4, y: 4 (y_hi: 2, y_lo: 2; y = y_hi * 2 + y_lo), z: 8, core: 2. Of those that a mesh axis runs over, the one named last changes fastest.
Arguments:
- features: bfloat16 [512, 32768], P(None, 'dom'), may hold values from -6 to 6
- weight: bfloat16 [512, 512], P(None, 'hid'), may hold values from -0.25 to 0.25
- band_tiles: bfloat16 [3072, 32768], P(None, 'dom'), may hold values from -0.109375 to 0.109375
- tile_live: int32 [12, 128], P(None, 'dom'), may hold values 0 or 1
- send_rows: int32 [32, 32, 128], P('dom'), may hold values from 0 to 1023
- recv_rows: int32 [32, 32, 128], P('dom'), may hold values from 0 to 1023
- edge_weight: float32 [32, 32, 128], P('dom'), may hold values from 0.25 to 1
- live_slots: int32 [32, 32], P('dom'), may hold values from 96 to 128, as said below
- bias_terms: float32 [512], P('hid'), may hold values from -3 to 3
- cotangent: bfloat16 [512, 32768], P('hid', 'dom'), may hold values from -6 to 6
Outputs:
- output: bfloat16 [512, 32768], P('hid', 'dom')
- feature_grad: bfloat16 [512, 32768], P('hid', 'dom')
- weight_grad: float32 [512, 512], P(None, 'hid')
- bias_grad: float32 [512], P('hid')
The draws below stay inside these ranges and needn't reach their ends.
Inputs may be any that keep to these rules, and one draw needn't show every extreme that they name: `live_slots`: every reader block has at least one owner block whose list has all 128 slots live.
All inputs are finite; a program needn't handle non-finite values. No bound on the sum of `tile_live` on one device may be relied on, other than what follows from the above.
Results may differ from the reference program's by a relative error of at most 0.0065.
Values may be sent and summed in bfloat16 or wider, within the bound.
A program may use at most 64 MiB of HBM per device.

```python
import math
import jax
import jax.numpy as jnp
from jax import lax

F = 512
H = 512
TILE = 256
C = 128
R_DEV = 1024
N = 32768
PEERS = 32
N_DOM = 32


def draw_live_slots(key, part):
    base = jax.random.randint(jax.random.fold_in(key, 11), (PEERS, PEERS), 3 * C // 4, C + 1)
    full_at = jax.random.randint(jax.random.fold_in(key, 12), (PEERS,), 0, PEERS)
    column = jnp.arange(PEERS)[None, :]
    return jnp.where(column == full_at[:, None], C, base).astype(jnp.int32)


def with_ends(result, key, smallest, high):
    longest = result.shape.index(max(result.shape))
    spots = []
    for shift in (0, 1):
        where = [jax.random.randint(jax.random.fold_in(key, axis), (), 0, length) for axis, length in enumerate(result.shape)]
        where[longest] = (where[longest] + shift) % result.shape[longest]
        spots.append(tuple(where))
    return result.at[spots[0]].set(smallest).at[spots[1]].set(high)


def levels(rng, extent, pieces, low, high):
    def one(dim, parts):
        draws = jax.random.uniform(jax.random.fold_in(jax.random.fold_in(rng, 6), dim), (parts,), jnp.float32, low / len(pieces), high / len(pieces))
        return jnp.repeat(jnp.exp(draws), extent[dim] // parts).reshape((-1,) + (1,) * (len(extent) - dim - 1))

    factor_of = one(*pieces[0])
    for cut in pieces[1:]:
        factor_of = factor_of * one(*cut)
    return factor_of


def noise(key, dims, spread, bound, split=(), kind=jnp.bfloat16):
    values = spread * jax.random.normal(key, dims, jnp.float32)
    if split:
        values = values * levels(key, dims, split, -0.22, 0.18)
    return jnp.clip(values, -bound, bound).astype(kind)


def setup_inputs(seed: int = 0) -> dict:
    seeds = jax.random.split(jax.random.key(seed), 11)
    return {
        "features": noise(seeds[0], (F, N), 1.0, 6.0, ((1, 32),)),
        "weight": noise(seeds[1], (F, H), F ** -0.5, 0.25, ((1, 8),)),
        "band_tiles": noise(seeds[2], (3 * R_DEV, N), (3 * R_DEV) ** -0.5, 0.109375, ((1, 32),)),
        "tile_live": with_ends((jax.random.randint(seeds[3], (3 * R_DEV // TILE, N // TILE), 0, 4) < 3).astype(jnp.int32), jax.random.fold_in(seeds[3], 1), 0, 1),
        "send_rows": with_ends(jax.random.randint(seeds[4], (PEERS, PEERS, C), 0, R_DEV), jax.random.fold_in(seeds[4], 1), 0, R_DEV - 1).astype(jnp.int32),
        "recv_rows": with_ends(jax.random.randint(seeds[5], (PEERS, PEERS, C), 0, R_DEV), jax.random.fold_in(seeds[5], 1), 0, R_DEV - 1).astype(jnp.int32),
        "edge_weight": jnp.clip(jnp.exp(math.log(1.0) - 1.3862944 * jax.random.uniform(seeds[6], (PEERS, PEERS, C), jnp.float32) ** levels(seeds[6], (PEERS, PEERS, C), ((0, 32),), -0.2, 0.2)), 0.25, 1.0),
        "live_slots": draw_live_slots(jax.random.fold_in(seeds[10], 71), 0),
        "bias_terms": noise(seeds[8], (H,), 0.5, 3.0, ((0, 8),), jnp.float32),
        "cotangent": noise(seeds[9], (H, N), 1.0, 6.0, ((0, 8), (1, 32))),
    }


def silu_grad(value):
    gate = jax.nn.sigmoid(value)
    return gate * (1.0 + value * (1.0 - gate))

def reference(features, weight, band_tiles, tile_live, send_rows, recv_rows, edge_weight, live_slots, bias_terms, cotangent):
    part_count = N_DOM
    row_count = R_DEV
    mapped = jnp.dot(weight.T, features, preferred_element_type=jnp.float32).astype(jnp.bfloat16)
    tile_mask = tile_live.astype(jnp.bfloat16)
    dense = (band_tiles.reshape(3 * row_count // TILE, TILE, part_count * row_count // TILE, TILE) * tile_mask[:, None, :, None]).reshape(3 * row_count, part_count * row_count)
    dense_f = dense.astype(jnp.float32).reshape(3, row_count, part_count, row_count)
    mapped_f = mapped.astype(jnp.float32)
    blocks = mapped_f.reshape(H, part_count, row_count)
    dense_sum = jnp.zeros((H, part_count, row_count), jnp.float32)
    for offset in range(3):
        source = jnp.roll(blocks, -(offset - 1), axis=1)
        dense_sum = dense_sum + jnp.einsum('hdj,jdi->hdi', source, dense_f[offset])
    slot_ids = jnp.arange(C)[None, None, :]
    slot_weight = edge_weight * (slot_ids < live_slots[:, :, None]).astype(jnp.float32)
    pick_order = jnp.transpose(send_rows, (1, 0, 2))
    send_cols = (jnp.arange(part_count)[None, :, None] * row_count + pick_order).reshape(-1)
    recv_cols = (jnp.arange(part_count)[:, None, None] * row_count + recv_rows).reshape(-1)
    flat_weight = slot_weight.reshape(-1)
    values = mapped_f[:, send_cols] * flat_weight[None, :]
    sparse_sum = jnp.zeros((H, part_count * row_count), jnp.float32).at[:, recv_cols].add(values)
    act = dense_sum.reshape(H, part_count * row_count) + sparse_sum + bias_terms[:, None]
    output = jax.nn.silu(act).astype(jnp.bfloat16)
    pre_grad = (cotangent.astype(jnp.float32) * silu_grad(act)).astype(jnp.bfloat16)
    grad_f = pre_grad.astype(jnp.float32)
    grad_blocks = grad_f.reshape(H, part_count, row_count)
    map_grad = jnp.zeros((H, part_count, row_count), jnp.float32)
    for offset in range(3):
        term = jnp.einsum('hdi,jdi->hdj', grad_blocks, dense_f[offset])
        map_grad = map_grad + jnp.roll(term, offset - 1, axis=1)
    message = (grad_f[:, recv_cols] * flat_weight[None, :]).astype(jnp.bfloat16)
    map_grad = map_grad.reshape(H, part_count * row_count).at[:, send_cols].add(message.astype(jnp.float32))
    grad_b = map_grad.astype(jnp.bfloat16)
    weight_grad = jnp.dot(features, grad_b.T, preferred_element_type=jnp.float32)
    bias_grad = lax.optimization_barrier(jnp.sum(grad_f, axis=1))
    feature_grad = jnp.dot(weight, grad_b, preferred_element_type=jnp.float32).astype(jnp.bfloat16)
    return (output, feature_grad, weight_grad, bias_grad)
```

```python
import functools

import jax
import jax.numpy as jnp
from jax import lax
from jax.experimental import pallas as pl
from jax.experimental.pallas import tpu as pltpu
from jax.sharding import PartitionSpec as P

MESH = pl.DeviceIdType.MESH
F32 = jnp.float32
BF16 = jnp.bfloat16
TILE = 256
NT = (((1,), (1,)), ((), ()))
ZS = 8
CHIPS = 16
BLOCKS = 32
HIDS = 8


def dot(a, b):
    return jnp.dot(a, b, preferred_element_type=F32)


def dot_nt(a, b):
    return lax.dot_general(a, b, NT, preferred_element_type=F32)


def row_to_column(row, rows):
    lanes = row.shape[1]
    at = lax.broadcasted_iota(jnp.int32, (rows, lanes), 0)
    to = lax.broadcasted_iota(jnp.int32, (rows, lanes), 1)
    return jnp.sum(jnp.where(at == to, row, 0.0), axis=1, keepdims=True)


def kernel(
    wt_ref,
    feat_hbm,
    band_hbm,
    live_ref,
    send_ref,
    recv_ref,
    ew_ref,
    slots_ref,
    bias_ref,
    cot_hbm,
    out_ref,
    fg_ref,
    wg_ref,
    bg_ref,
    feat,
    band,
    cot,
    mapped,
    near,
    picks,
    puts,
    weights,
    acc,
    pre,
    term,
    term_in,
    out1,
    in1,
    out2,
    in2,
    wsend,
    wrecv,
    wfull,
    gb,
    bias_out,
    bias_in,
    pieces,
    pieces_in,
    summed,
    wg_all,
    load_sem,
    a1_send,
    a1_recv,
    n1_send,
    n1_recv,
    a2_send,
    a2_recv,
    n2_send,
    n2_recv,
    w_send,
    w_recv,
    b_send,
    b_recv,
    g_send,
    g_recv,
    rs_send,
    rs_recv,
    ag_send,
    ag_recv,
):
    me = lax.axis_index("dom")
    hid = lax.axis_index("hid")
    core = lax.rem(me, 2)
    z = lax.rem(me // 2, ZS)
    yh = me // (2 * ZS)
    left = lax.rem(me + BLOCKS - 1, BLOCKS)
    right = lax.rem(me + 1, BLOCKS)
    rows = mapped.shape[1]
    width = mapped.shape[0]

    def remote(src, dst, ssem, rsem, **where):
        return pltpu.make_async_remote_copy(
            src_ref=src, dst_ref=dst, send_sem=ssem, recv_sem=rsem,
            device_id=where, device_id_type=MESH,
        )

    def place(k):
        step = k // 2
        half = (step + 1) // 2
        dz = lax.rem(4 + half * (1 - 2 * lax.rem(step, 2)) + ZS, ZS)
        dy = 1 - lax.rem(k, 2)
        slot = 2 * dz + dy
        back = 2 * lax.rem(ZS - dz, ZS) + dy
        chip = lax.rem(yh + dy, 2) * ZS + lax.rem(z + dz, ZS)
        return slot, back, chip

    feat_copy = pltpu.make_async_copy(feat_hbm, feat, load_sem.at[0])
    band_copy = pltpu.make_async_copy(band_hbm, band, load_sem.at[1])
    cot_copy = pltpu.make_async_copy(cot_hbm, cot, load_sem.at[2])
    feat_copy.start()
    band_copy.start()
    cot_copy.start()

    barrier = pltpu.get_barrier_semaphore()

    @pl.loop(1, BLOCKS)
    def _(j):
        pl.semaphore_signal(barrier, inc=1, device_id={"dom": lax.rem(me + j, BLOCKS)}, device_id_type=MESH)

    @pl.loop(1, HIDS)
    def _(j):
        pl.semaphore_signal(barrier, inc=1, device_id={"hid": lax.rem(hid + j, HIDS)}, device_id_type=MESH)

    slot_ids = lax.broadcasted_iota(jnp.int32, (BLOCKS, 128), 1).astype(F32)
    counts = row_to_column(slots_ref[...].astype(F32), BLOCKS)
    weights[...] = jnp.where(slot_ids < counts, ew_ref[...], 0.0)
    wt = wt_ref[...]
    wsend[...] = jnp.zeros_like(wsend)
    for p in range(HIDS):
        wsend[p, :, :width] = wt[:, p * width:(p + 1) * width]
    wrecv[0] = wsend[hid]

    feat_copy.wait()

    @pl.loop(0, rows // TILE)
    def _(j):
        cols = pl.ds(pl.multiple_of(j * TILE, TILE), TILE)
        mapped[:, cols] = dot(wt_ref[...], feat[:, cols]).astype(BF16)

    pl.semaphore_wait(barrier, BLOCKS - 1 + HIDS - 1)

    to_right = remote(mapped, near.at[0], n1_send.at[0], n1_recv.at[0], dom=right)
    to_left = remote(mapped, near.at[1], n1_send.at[1], n1_recv.at[1], dom=left)
    to_right.start()
    to_left.start()

    def onehot(ref, chip):
        index = jnp.concatenate(
            [ref[pl.ds(2 * chip, 1), :], ref[pl.ds(2 * chip + 1, 1), :]], axis=1
        )
        at = lax.broadcasted_iota(jnp.int32, (rows, 2 * 128), 0)
        return jnp.where(at == index, 1.0, 0.0).astype(BF16)

    def slot_row(chip):
        return jnp.concatenate(
            [weights[pl.ds(2 * chip, 1), :], weights[pl.ds(2 * chip + 1, 1), :]], axis=1
        )

    def pick(slot, chip):
        picks[slot] = onehot(send_ref, chip)
        got = dot(mapped[...], picks[slot]).astype(BF16)
        out1[slot, 0] = got[:, :128]
        out1[slot, 1] = got[:, 128:]

    def ship(outs, ins, ssem, rsem, slot, back, chip, h):
        return remote(
            outs.at[slot, h], ins.at[back, core], ssem.at[slot, h], rsem.at[back, core],
            dom=2 * chip + h,
        )

    own = yh * ZS + z

    @pl.loop(0, CHIPS - 1)
    def _(k):
        slot, back, chip = place(k)
        pick(slot, chip)
        for h in range(2):
            ship(out1, in1, a1_send, a1_recv, slot, back, chip, h).start()

    pick(0, own)
    ship(out1, in1, a1_send, a1_recv, 0, 0, own, 1 - core).start()
    in1[0, core] = out1[0, core]

    @pl.loop(1, HIDS)
    def _(j):
        peer = lax.rem(hid + j, HIDS)
        remote(wsend.at[peer], wrecv.at[HIDS - j], w_send.at[j], w_recv.at[HIDS - j], hid=peer).start()

    band_copy.wait()

    def dense_forward(source, s):
        @pl.loop(0, rows // TILE)
        def _(j):
            cols = pl.ds(pl.multiple_of(j * TILE, TILE), TILE)
            parts = [
                (source[:, t * TILE:(t + 1) * TILE].astype(F32)
                 * live_ref[j, s * 4 + t].astype(F32)).astype(BF16)
                for t in range(rows // TILE)
            ]
            got = dot(jnp.concatenate(parts, axis=1), band[s * rows:(s + 1) * rows, cols])
            if s == 1:
                acc[:, cols] = got
            else:
                acc[:, cols] += got

    dense_forward(mapped, 1)

    @pl.loop(0, CHIPS)
    def _(k):
        slot, _, chip = place(k)
        puts[slot] = onehot(recv_ref, chip)

    to_right.wait_recv()
    dense_forward(near.at[0], 0)
    to_left.wait_recv()
    dense_forward(near.at[1], 2)

    def put(slot, chip):
        pair = jnp.concatenate([in1[slot, 0], in1[slot, 1]], axis=1).astype(F32)
        acc[...] += dot_nt((pair * slot_row(chip)).astype(BF16), puts[slot])

    remote(out1.at[0, 0], in1.at[0, 1 - core], a1_send.at[0, 0], a1_recv.at[0, 1 - core], dom=left).wait_recv()
    put(0, own)

    @pl.loop(0, CHIPS - 1)
    def _(k):
        slot, _, chip = place(k)
        for h in range(2):
            remote(out1.at[slot, h], in1.at[slot, h], a1_send.at[slot, h], a1_recv.at[slot, h], dom=left).wait_recv()
        put(slot, chip)

    cot_copy.wait()
    act = acc[...] + row_to_column(bias_ref[...], width)
    gate = 1.0 / (1.0 + jnp.exp(-act))
    out_ref[...] = (act * gate).astype(BF16)
    grad = (cot[...].astype(F32) * (gate * (1.0 + act * (1.0 - gate)))).astype(BF16)
    pre[...] = grad
    bias_col = jnp.sum(grad.astype(F32), axis=1, keepdims=True)
    diagonal = lax.broadcasted_iota(jnp.int32, (width, 128), 0) == lax.broadcasted_iota(jnp.int32, (width, 128), 1)
    bias_row = jnp.sum(jnp.where(diagonal, bias_col, 0.0), axis=0, keepdims=True)
    bias_out[0] = jnp.broadcast_to(bias_row, (8, 128))

    def bias_peer(step):
        bit = 1 << step
        return me + bit * (1 - 2 * lax.rem(me // bit, 2))

    def bias_copy(step):
        return remote(bias_out.at[step], bias_in.at[step], b_send.at[step], b_recv.at[step], dom=bias_peer(step))

    def bias_step(step):
        bias_copy(step).wait_recv()
        total = bias_out[step] + bias_in[step]
        bias_out[step + 1] = total
        if step < 4:
            bias_copy(step + 1).start()

    bias_copy(0).start()

    def message(slot, chip):
        got = (dot(pre[...], puts[slot]) * slot_row(chip)).astype(BF16)
        out2[slot, 0] = got[:, :128]
        out2[slot, 1] = got[:, 128:]

    def send_messages(lo, hi):
        @pl.loop(lo, hi)
        def _(k):
            slot, back, chip = place(k)
            message(slot, chip)
            for h in range(2):
                ship(out2, in2, a2_send, a2_recv, slot, back, chip, h).start()

    def dense_backward(target, s):
        @pl.loop(0, rows // TILE)
        def _(t):
            cols = pl.ds(pl.multiple_of(t * TILE, TILE), TILE)
            parts = [
                (pre[:, j * TILE:(j + 1) * TILE].astype(F32)
                 * live_ref[j, s * 4 + t].astype(F32)).astype(BF16)
                for j in range(rows // TILE)
            ]
            band_rows = pl.ds(pl.multiple_of(s * rows + t * TILE, TILE), TILE)
            got = dot_nt(jnp.concatenate(parts, axis=1), band[band_rows, :])
            target[:, cols] = got.astype(target.dtype)

    send_messages(0, 6)
    dense_backward(term.at[0], 0)
    grad_left = remote(term.at[0], term_in.at[0], n2_send.at[0], n2_recv.at[0], dom=left)
    grad_left.start()
    dense_backward(term.at[1], 2)
    grad_right = remote(term.at[1], term_in.at[1], n2_send.at[1], n2_recv.at[1], dom=right)
    grad_right.start()
    send_messages(6, CHIPS - 1)
    message(0, own)
    ship(out2, in2, a2_send, a2_recv, 0, 0, own, 1 - core).start()
    in2[0, core] = out2[0, core]
    bias_step(0)

    dense_backward(acc, 1)

    @pl.loop(1, HIDS)
    def _(j):
        remote(wsend.at[j], wrecv.at[j], w_send.at[j], w_recv.at[j], dom=left).wait_recv()

    wfull[...] = jnp.transpose(
        wrecv[...].reshape(HIDS * width, 128).astype(F32), (1, 0)
    )[:width].astype(BF16)

    grad_left.wait_recv()
    grad_right.wait_recv()
    acc[...] += term_in[0].astype(F32) + term_in[1].astype(F32)

    def give_back(slot):
        pair = jnp.concatenate([in2[slot, 0], in2[slot, 1]], axis=1)
        acc[...] += dot_nt(pair, picks[slot])

    remote(out2.at[0, 0], in2.at[0, 1 - core], a2_send.at[0, 0], a2_recv.at[0, 1 - core], dom=left).wait_recv()
    give_back(0)

    @pl.loop(0, CHIPS - 1)
    def _(k):
        slot, _, chip = place(k)
        for h in range(2):
            remote(out2.at[slot, h], in2.at[slot, h], a2_send.at[slot, h], a2_recv.at[slot, h], dom=left).wait_recv()
        give_back(slot)

    gb[0] = acc[...].astype(BF16)

    @pl.loop(1, HIDS)
    def _(j):
        remote(gb.at[0], gb.at[HIDS - j], g_send.at[j], g_recv.at[HIDS - j], hid=lax.rem(hid + j, HIDS)).start()

    wg = dot_nt(gb[0], feat[...])
    for d in range(BLOCKS):
        r, c = d // 4, d % 4
        pieces[d] = wg[8 * r:8 * r + 8, 128 * c:128 * c + 128]

    @pl.loop(1, BLOCKS)
    def _(j):
        peer = lax.rem(me + j, BLOCKS)
        remote(pieces.at[peer], pieces_in.at[BLOCKS - j], rs_send.at[j], rs_recv.at[BLOCKS - j], dom=peer).start()

    bias_step(1)
    bias_step(2)

    summed[...] = pieces[me]

    @pl.loop(1, BLOCKS)
    def _(j):
        remote(pieces.at[j], pieces_in.at[j], rs_send.at[j], rs_recv.at[j], dom=left).wait_recv()
        summed[...] += pieces_in[j]

    @pl.loop(1, BLOCKS)
    def _(j):
        peer = lax.rem(me + j, BLOCKS)
        remote(summed, wg_all.at[me], ag_send.at[j], ag_recv.at[BLOCKS - j], dom=peer).start()

    wg_all[me] = summed[...]
    bias_step(3)
    bias_step(4)
    bg_ref[...] = bias_out[5, 0:1, :width]

    @pl.loop(1, HIDS)
    def _(j):
        remote(gb.at[0], gb.at[j], g_send.at[j], g_recv.at[j], dom=left).wait_recv()

    @pl.loop(0, rows // TILE)
    def _(j):
        cols = pl.ds(pl.multiple_of(j * TILE, TILE), TILE)
        stack = gb[:, :, cols].reshape(HIDS * width, TILE)
        fg_ref[:, cols] = dot(wfull[...], stack).astype(BF16)

    @pl.loop(1, BLOCKS)
    def _(j):
        remote(summed, wg_all.at[lax.rem(me + j, BLOCKS)], ag_send.at[j], ag_recv.at[j], dom=left).wait_recv()

    for d in range(BLOCKS):
        r, c = d // 4, d % 4
        wg_ref[8 * r:8 * r + 8, 128 * c:128 * c + 128] = wg_all[d]

    to_right.wait_send()
    to_left.wait_send()
    grad_left.wait_send()
    grad_right.wait_send()
    for step in range(5):
        bias_copy(step).wait_send()

    @pl.loop(0, CHIPS - 1)
    def _(k):
        slot, back, chip = place(k)
        for h in range(2):
            ship(out1, in1, a1_send, a1_recv, slot, back, chip, h).wait_send()
            ship(out2, in2, a2_send, a2_recv, slot, back, chip, h).wait_send()

    ship(out1, in1, a1_send, a1_recv, 0, 0, own, 1 - core).wait_send()
    ship(out2, in2, a2_send, a2_recv, 0, 0, own, 1 - core).wait_send()

    @pl.loop(1, HIDS)
    def _(j):
        peer = lax.rem(hid + j, HIDS)
        remote(wsend.at[peer], wrecv.at[HIDS - j], w_send.at[j], w_recv.at[HIDS - j], hid=peer).wait_send()
        remote(gb.at[0], gb.at[HIDS - j], g_send.at[j], g_recv.at[HIDS - j], hid=peer).wait_send()

    @pl.loop(1, BLOCKS)
    def _(j):
        peer = lax.rem(me + j, BLOCKS)
        remote(pieces.at[peer], pieces_in.at[BLOCKS - j], rs_send.at[j], rs_recv.at[BLOCKS - j], dom=peer).wait_send()
        remote(summed, wg_all.at[me], ag_send.at[j], ag_recv.at[BLOCKS - j], dom=peer).wait_send()


def on_device(
    features,
    weight,
    band_tiles,
    tile_live,
    send_rows,
    recv_rows,
    edge_weight,
    live_slots,
    bias_terms,
    cotangent,
):
    depth, rows = features.shape
    width = weight.shape[1]
    vmem = pl.BlockSpec(memory_space=pltpu.VMEM)
    hbm = pl.BlockSpec(memory_space=pl.ANY)
    smem = pl.BlockSpec(memory_space=pltpu.SMEM)
    dma = pltpu.SemaphoreType.DMA
    block = pltpu.VMEM((width, rows), BF16)
    lists = pltpu.VMEM((CHIPS, 2, width, 128), BF16)
    output, feature_grad, wg, bg = pl.pallas_call(
        kernel,
        out_shape=(
            jax.ShapeDtypeStruct((width, rows), BF16),
            jax.ShapeDtypeStruct((width, rows), BF16),
            jax.ShapeDtypeStruct((width, depth), F32),
            jax.ShapeDtypeStruct((1, width), F32),
        ),
        in_specs=[vmem, hbm, hbm, smem, vmem, vmem, vmem, vmem, vmem, hbm],
        out_specs=(vmem,) * 4,
        scratch_shapes=[
            pltpu.VMEM((depth, rows), BF16),
            pltpu.VMEM((3 * rows, rows), BF16),
            block,
            block,
            pltpu.VMEM((2, width, rows), BF16),
            pltpu.VMEM((CHIPS, rows, 256), BF16),
            pltpu.VMEM((CHIPS, rows, 256), BF16),
            pltpu.VMEM((BLOCKS, 128), F32),
            pltpu.VMEM((width, rows), F32),
            block,
            pltpu.VMEM((2, width, rows), BF16),
            pltpu.VMEM((2, width, rows), BF16),
            lists,
            lists,
            lists,
            lists,
            pltpu.VMEM((HIDS, width, 128), BF16),
            pltpu.VMEM((HIDS, width, 128), BF16),
            pltpu.VMEM((width, HIDS * width), BF16),
            pltpu.VMEM((HIDS, width, rows), BF16),
            pltpu.VMEM((6, 8, 128), F32),
            pltpu.VMEM((5, 8, 128), F32),
            pltpu.VMEM((BLOCKS, 8, 128), F32),
            pltpu.VMEM((BLOCKS, 8, 128), F32),
            pltpu.VMEM((8, 128), F32),
            pltpu.VMEM((BLOCKS, 8, 128), F32),
            dma((3,)),
            dma((CHIPS, 2)),
            dma((CHIPS, 2)),
            dma((2,)),
            dma((2,)),
            dma((CHIPS, 2)),
            dma((CHIPS, 2)),
            dma((2,)),
            dma((2,)),
            dma((HIDS,)),
            dma((HIDS,)),
            dma((5,)),
            dma((5,)),
            dma((HIDS,)),
            dma((HIDS,)),
            dma((BLOCKS,)),
            dma((BLOCKS,)),
            dma((BLOCKS,)),
            dma((BLOCKS,)),
        ],
        compiler_params=pltpu.CompilerParams(
            collective_id=0, has_side_effects=True, vmem_limit_bytes=56 << 20
        ),
    )(
        weight.T,
        features,
        band_tiles,
        tile_live.T,
        send_rows[0],
        recv_rows[0],
        edge_weight[0],
        live_slots,
        bias_terms.reshape(1, width),
        cotangent,
    )
    return (output, feature_grad, wg.T, bg.reshape(width))


def solution(mesh):
    return jax.shard_map(
        on_device,
        mesh=mesh,
        in_specs=(
            P(None, "dom"),
            P(None, "hid"),
            P(None, "dom"),
            P(None, "dom"),
            P("dom", None, None),
            P("dom", None, None),
            P("dom", None, None),
            P("dom", None),
            P("hid"),
            P("hid", "dom"),
        ),
        out_specs=(P("hid", "dom"), P("hid", "dom"), P(None, "hid"), P("hid")),
        check_vma=False,
    )
```

```python
import jax
import jax.numpy as jnp
from jax import lax
from jax.experimental import pallas as pl
from jax.experimental.pallas import tpu as pltpu
from jax.sharding import PartitionSpec as P

MESH = pl.DeviceIdType.MESH
F32 = jnp.float32
BF16 = jnp.bfloat16
TILE = 256
NT = (((1,), (1,)), ((), ()))
ZS = 8
CHIPS = 16
BLOCKS = 32
HIDS = 8


def dot(a, b):
    return jnp.dot(a, b, preferred_element_type=F32)


def dot_nt(a, b):
    return lax.dot_general(a, b, NT, preferred_element_type=F32)


def row_to_column(row, rows):
    lanes = row.shape[1]
    at = lax.broadcasted_iota(jnp.int32, (rows, lanes), 0)
    to = lax.broadcasted_iota(jnp.int32, (rows, lanes), 1)
    return jnp.sum(jnp.where(at == to, row, 0.0), axis=1, keepdims=True)


def kernel(
    wt_hbm,
    feat_hbm,
    band_hbm,
    live_hbm,
    send_hbm,
    recv_hbm,
    ew_hbm,
    slots_hbm,
    bias_hbm,
    cot_hbm,
    out_ref,
    fg_ref,
    wg_ref,
    bg_ref,
    wt_ref,
    feat,
    band,
    live_ref,
    send_ref,
    recv_ref,
    ew_ref,
    slots_ref,
    bias_ref,
    cot,
    mapped,
    near,
    picks,
    puts,
    weights,
    acc,
    pre,
    term,
    term_in,
    out1,
    in1,
    out2,
    in2,
    wsend,
    wrecv,
    wfull,
    gb,
    bias_out,
    bias_in,
    pieces,
    pieces_in,
    summed,
    wg_all,
    load_sem,
    a1_send,
    a1_recv,
    n1_send,
    n1_recv,
    a2_send,
    a2_recv,
    n2_send,
    n2_recv,
    w_send,
    w_recv,
    b_send,
    b_recv,
    g_send,
    g_recv,
    rs_send,
    rs_recv,
    ag_send,
    ag_recv,
):
    me = lax.axis_index("dom")
    hid = lax.axis_index("hid")
    core = lax.rem(me, 2)
    z = lax.rem(me // 2, ZS)
    yh = me // (2 * ZS)
    own = yh * ZS + z
    left = lax.rem(me + BLOCKS - 1, BLOCKS)
    right = lax.rem(me + 1, BLOCKS)
    rows = mapped.shape[1]
    width = mapped.shape[0]
    half = width // 2
    barrier = pltpu.get_barrier_semaphore()

    @pl.loop(1, BLOCKS)
    def _(j):
        pl.semaphore_signal(barrier, inc=1, device_id={"dom": lax.rem(me + j, BLOCKS)}, device_id_type=MESH)

    @pl.loop(1, HIDS)
    def _(j):
        pl.semaphore_signal(barrier, inc=1, device_id={"hid": lax.rem(hid + j, HIDS)}, device_id_type=MESH)

    loads = [
        pltpu.make_async_copy(src, dst, load_sem.at[i])
        for i, (src, dst) in enumerate((
            (wt_hbm, wt_ref), (feat_hbm, feat), (send_hbm, send_ref), (slots_hbm, slots_ref),
            (ew_hbm, ew_ref), (recv_hbm, recv_ref), (bias_hbm, bias_ref), (live_hbm, live_ref),
            (band_hbm, band), (cot_hbm, cot),
        ))
    ]
    for load in loads:
        load.start()

    def remote(src, dst, ssem, rsem, **where):
        return pltpu.make_async_remote_copy(
            src_ref=src, dst_ref=dst, send_sem=ssem, recv_sem=rsem,
            device_id=where, device_id_type=MESH,
        )

    def place(k):
        step = k // 2
        far = (step + 1) // 2
        dz = lax.rem(4 + far * (1 - 2 * lax.rem(step, 2)) + ZS, ZS)
        dy = 1 - lax.rem(k, 2)
        slot = 2 * dz + dy
        back = 2 * lax.rem(ZS - dz, ZS) + dy
        chip = lax.rem(yh + dy, 2) * ZS + lax.rem(z + dz, ZS)
        return slot, back, chip

    for load in loads[:4]:
        load.wait()

    @pl.loop(0, rows // TILE)
    def _(j):
        cols = pl.ds(pl.multiple_of(j * TILE, TILE), TILE)
        mapped[:, cols] = dot(wt_ref[...], feat[:, cols]).astype(BF16)

    pl.semaphore_wait(barrier, BLOCKS - 1 + HIDS - 1)

    to_right = remote(mapped, near.at[0], n1_send.at[0], n1_recv.at[0], dom=right)
    to_left = remote(mapped, near.at[1], n1_send.at[1], n1_recv.at[1], dom=left)
    to_right.start()
    to_left.start()

    def onehot(ref, chip):
        index = jnp.concatenate(
            [ref[pl.ds(2 * chip, 1), :], ref[pl.ds(2 * chip + 1, 1), :]], axis=1
        )
        at = lax.broadcasted_iota(jnp.int32, (rows, 2 * 128), 0)
        return jnp.where(at == index, 1.0, 0.0).astype(BF16)

    def slot_row(chip):
        return jnp.concatenate(
            [weights[pl.ds(2 * chip, 1), :], weights[pl.ds(2 * chip + 1, 1), :]], axis=1
        )

    def pick(slot, chip):
        picks[slot] = onehot(send_ref, chip)
        got = dot(mapped[...], picks[slot]).astype(BF16)
        for h in range(2):
            for c in range(2):
                out1[h, slot, c] = got[h * half:(h + 1) * half, c * 128:(c + 1) * 128]

    def ship(first, h, slot, back, chip, c):
        outs, ins, ssem, rsem = (out1, in1, a1_send, a1_recv) if first else (out2, in2, a2_send, a2_recv)
        return remote(
            outs.at[h, slot, c], ins.at[h, back, core], ssem.at[h, slot, c], rsem.at[h, back, core],
            dom=2 * chip + c,
        )

    def arrive(first, h, slot, c):
        outs, ins, ssem, rsem = (out1, in1, a1_send, a1_recv) if first else (out2, in2, a2_send, a2_recv)
        remote(
            outs.at[h, slot, c], ins.at[h, slot, c], ssem.at[h, slot, c], rsem.at[h, slot, c], dom=left
        ).wait_recv()

    @pl.loop(0, CHIPS - 1)
    def _(k):
        slot, back, chip = place(k)
        pick(slot, chip)
        for c in range(2):
            ship(True, 0, slot, back, chip, c).start()

    pick(0, own)
    for h in range(2):
        ship(True, h, 0, 0, own, 1 - core).start()
        in1[h, 0, core] = out1[h, 0, core]

    @pl.loop(0, CHIPS - 1)
    def _(k):
        slot, back, chip = place(k)
        for c in range(2):
            ship(True, 1, slot, back, chip, c).start()

    for load in loads[4:]:
        load.wait()

    wt = wt_ref[...]
    wsend[...] = jnp.zeros_like(wsend)
    for p in range(HIDS):
        wsend[p, :, :width] = wt[:, p * width:(p + 1) * width]
    wrecv[0] = wsend[hid]

    @pl.loop(1, HIDS)
    def _(j):
        peer = lax.rem(hid + j, HIDS)
        remote(wsend.at[peer], wrecv.at[HIDS - j], w_send.at[j], w_recv.at[HIDS - j], hid=peer).start()

    slot_ids = lax.broadcasted_iota(jnp.int32, (BLOCKS, 128), 1).astype(F32)
    counts = row_to_column(slots_ref[...].astype(F32), BLOCKS)
    weights[...] = jnp.where(slot_ids < counts, ew_ref[...], 0.0)

    def dense_forward(source, s):
        @pl.loop(0, rows // TILE)
        def _(j):
            cols = pl.ds(pl.multiple_of(j * TILE, TILE), TILE)
            parts = [
                (source[:, t * TILE:(t + 1) * TILE].astype(F32)
                 * live_ref[j, s * 4 + t].astype(F32)).astype(BF16)
                for t in range(rows // TILE)
            ]
            got = dot(jnp.concatenate(parts, axis=1), band[s * rows:(s + 1) * rows, cols])
            if s == 1:
                acc[:, cols] = got
            else:
                acc[:, cols] += got

    dense_forward(mapped, 1)

    @pl.loop(0, CHIPS)
    def _(k):
        slot, _, chip = place(k)
        puts[slot] = onehot(recv_ref, chip)

    to_right.wait_recv()
    dense_forward(near.at[0], 0)
    to_left.wait_recv()
    dense_forward(near.at[1], 2)

    bias_in_col = row_to_column(bias_ref[...], width)

    def put(h, slot, chip):
        pair = jnp.concatenate([in1[h, slot, 0], in1[h, slot, 1]], axis=1).astype(F32)
        acc[h * half:(h + 1) * half] += dot_nt((pair * slot_row(chip)).astype(BF16), puts[slot])

    def activate(h):
        part = slice(h * half, (h + 1) * half)
        arrive(True, h, 0, 1 - core)
        put(h, 0, own)

        @pl.loop(0, CHIPS - 1)
        def _(k):
            slot, _, chip = place(k)
            for c in range(2):
                arrive(True, h, slot, c)
            put(h, slot, chip)

        act = acc[part] + bias_in_col[part]
        gate = 1.0 / (1.0 + jnp.exp(-act))
        out_ref[part] = (act * gate).astype(BF16)
        pre[part] = (cot[part].astype(F32) * (gate * (1.0 + act * (1.0 - gate)))).astype(BF16)

    def message(h, slot, chip):
        got = (dot(pre[h * half:(h + 1) * half], puts[slot]) * slot_row(chip)).astype(BF16)
        out2[h, slot, 0] = got[:, :128]
        out2[h, slot, 1] = got[:, 128:]

    def send_messages(h):
        @pl.loop(0, CHIPS - 1)
        def _(k):
            slot, back, chip = place(k)
            message(h, slot, chip)
            for c in range(2):
                ship(False, h, slot, back, chip, c).start()

        message(h, 0, own)
        ship(False, h, 0, 0, own, 1 - core).start()
        in2[h, 0, core] = out2[h, 0, core]

    def dense_backward(target, s):
        @pl.loop(0, rows // TILE)
        def _(t):
            cols = pl.ds(pl.multiple_of(t * TILE, TILE), TILE)
            parts = [
                (pre[:, j * TILE:(j + 1) * TILE].astype(F32)
                 * live_ref[j, s * 4 + t].astype(F32)).astype(BF16)
                for j in range(rows // TILE)
            ]
            band_rows = pl.ds(pl.multiple_of(s * rows + t * TILE, TILE), TILE)
            got = dot_nt(jnp.concatenate(parts, axis=1), band[band_rows, :])
            target[:, cols] = got.astype(target.dtype)

    def bias_copy(step):
        bit = 1 << step
        peer = me + bit * (1 - 2 * lax.rem(me // bit, 2))
        return remote(bias_out.at[step], bias_in.at[step], b_send.at[step], b_recv.at[step], dom=peer)

    def bias_step(step):
        bias_copy(step).wait_recv()
        bias_out[step + 1] = bias_out[step] + bias_in[step]
        if step < 4:
            bias_copy(step + 1).start()

    activate(0)
    send_messages(0)
    activate(1)

    dense_backward(term.at[0], 0)
    grad_left = remote(term.at[0], term_in.at[0], n2_send.at[0], n2_recv.at[0], dom=left)
    grad_left.start()
    dense_backward(term.at[1], 2)
    grad_right = remote(term.at[1], term_in.at[1], n2_send.at[1], n2_recv.at[1], dom=right)
    grad_right.start()
    bias_col = jnp.sum(pre[...].astype(F32), axis=1, keepdims=True)
    diagonal = lax.broadcasted_iota(jnp.int32, (width, 128), 0) == lax.broadcasted_iota(jnp.int32, (width, 128), 1)
    bias_row = jnp.sum(jnp.where(diagonal, bias_col, 0.0), axis=0, keepdims=True)
    bias_out[0] = jnp.broadcast_to(bias_row, (8, 128))
    bias_copy(0).start()
    send_messages(1)
    bias_step(0)

    dense_backward(acc, 1)

    @pl.loop(1, HIDS)
    def _(j):
        remote(wsend.at[j], wrecv.at[j], w_send.at[j], w_recv.at[j], dom=left).wait_recv()

    wfull[...] = jnp.transpose(
        wrecv[...].reshape(HIDS * width, 128).astype(F32), (1, 0)
    )[:width].astype(BF16)

    grad_left.wait_recv()
    grad_right.wait_recv()
    acc[...] += term_in[0].astype(F32) + term_in[1].astype(F32)

    def give_back(h, slot):
        pair = jnp.concatenate([in2[h, slot, 0], in2[h, slot, 1]], axis=1)
        acc[h * half:(h + 1) * half] += dot_nt(pair, picks[slot])

    def gradient(h):
        arrive(False, h, 0, 1 - core)
        give_back(h, 0)

        @pl.loop(0, CHIPS - 1)
        def _(k):
            slot, _, chip = place(k)
            for c in range(2):
                arrive(False, h, slot, c)
            give_back(h, slot)

        part = slice(h * half, (h + 1) * half)
        gb[0, part] = acc[part].astype(BF16)

    def share(h, j):
        part = pl.ds(h * half, half)
        return remote(
            gb.at[0, part], gb.at[HIDS - j, part], g_send.at[h, j], g_recv.at[h, HIDS - j],
            hid=lax.rem(hid + j, HIDS),
        )

    def share_all(h):
        @pl.loop(1, HIDS)
        def _(j):
            share(h, j).start()

    gradient(0)
    share_all(0)
    gradient(1)

    wg = dot_nt(gb[0], feat[...])
    for d in range(BLOCKS):
        r, c = d // 4, d % 4
        pieces[d] = wg[8 * r:8 * r + 8, 128 * c:128 * c + 128]

    @pl.loop(1, BLOCKS)
    def _(j):
        peer = lax.rem(me + j, BLOCKS)
        remote(pieces.at[peer], pieces_in.at[BLOCKS - j], rs_send.at[j], rs_recv.at[BLOCKS - j], dom=peer).start()

    share_all(1)
    bias_step(1)
    summed[...] = pieces[me]

    @pl.loop(1, BLOCKS)
    def _(j):
        remote(pieces.at[j], pieces_in.at[j], rs_send.at[j], rs_recv.at[j], dom=left).wait_recv()
        summed[...] += pieces_in[j]

    @pl.loop(1, BLOCKS)
    def _(j):
        peer = lax.rem(me + j, BLOCKS)
        remote(summed, wg_all.at[me], ag_send.at[j], ag_recv.at[BLOCKS - j], dom=peer).start()

    wg_all[me] = summed[...]
    bias_step(2)
    bias_step(3)

    for h in range(2):
        @pl.loop(1, HIDS)
        def _(j):
            part = pl.ds(h * half, half)
            remote(gb.at[0, part], gb.at[j, part], g_send.at[h, j], g_recv.at[h, j], dom=left).wait_recv()

    @pl.loop(0, rows // TILE)
    def _(j):
        cols = pl.ds(pl.multiple_of(j * TILE, TILE), TILE)
        stack = gb[:, :, cols].reshape(HIDS * width, TILE)
        fg_ref[:, cols] = dot(wfull[...], stack).astype(BF16)

    bias_step(4)
    bg_ref[...] = bias_out[5, 0:1, :width]

    @pl.loop(1, BLOCKS)
    def _(j):
        remote(summed, wg_all.at[lax.rem(me + j, BLOCKS)], ag_send.at[j], ag_recv.at[j], dom=left).wait_recv()

    for d in range(BLOCKS):
        r, c = d // 4, d % 4
        wg_ref[8 * r:8 * r + 8, 128 * c:128 * c + 128] = wg_all[d]

    to_right.wait_send()
    to_left.wait_send()
    grad_left.wait_send()
    grad_right.wait_send()
    for step in range(5):
        bias_copy(step).wait_send()

    @pl.loop(0, CHIPS - 1)
    def _(k):
        slot, back, chip = place(k)
        for h in range(2):
            for c in range(2):
                ship(True, h, slot, back, chip, c).wait_send()
                ship(False, h, slot, back, chip, c).wait_send()

    for h in range(2):
        ship(True, h, 0, 0, own, 1 - core).wait_send()
        ship(False, h, 0, 0, own, 1 - core).wait_send()

    @pl.loop(1, HIDS)
    def _(j):
        peer = lax.rem(hid + j, HIDS)
        remote(wsend.at[peer], wrecv.at[HIDS - j], w_send.at[j], w_recv.at[HIDS - j], hid=peer).wait_send()
        for h in range(2):
            share(h, j).wait_send()

    @pl.loop(1, BLOCKS)
    def _(j):
        peer = lax.rem(me + j, BLOCKS)
        remote(pieces.at[peer], pieces_in.at[BLOCKS - j], rs_send.at[j], rs_recv.at[BLOCKS - j], dom=peer).wait_send()
        remote(summed, wg_all.at[me], ag_send.at[j], ag_recv.at[BLOCKS - j], dom=peer).wait_send()


def finish(*refs):
    sources, targets, sem = refs[:4], refs[4:8], refs[8]
    copies = [
        pltpu.make_async_copy(src, dst, sem.at[i])
        for i, (src, dst) in enumerate(zip(sources, targets))
    ]
    for copy in copies:
        copy.start()
    for copy in copies:
        copy.wait()


def on_device(
    features,
    weight,
    band_tiles,
    tile_live,
    send_rows,
    recv_rows,
    edge_weight,
    live_slots,
    bias_terms,
    cotangent,
):
    depth, rows = features.shape
    width = weight.shape[1]
    vmem = pl.BlockSpec(memory_space=pltpu.VMEM)
    hbm = pl.BlockSpec(memory_space=pltpu.HBM)
    dma = pltpu.SemaphoreType.DMA
    block = pltpu.VMEM((width, rows), BF16)
    lists = pltpu.VMEM((2, CHIPS, 2, width // 2, 128), BF16)
    results = (((width, rows), BF16), ((width, rows), BF16), ((width, depth), F32), ((1, width), F32))
    parts = pl.pallas_call(
        kernel,
        out_shape=tuple(pltpu.VMEM(*r) for r in results),
        in_specs=[hbm] * 10,
        out_specs=(vmem,) * 4,
        scratch_shapes=[
            pltpu.VMEM((width, depth), BF16),
            pltpu.VMEM((depth, rows), BF16),
            pltpu.VMEM((3 * rows, rows), BF16),
            pltpu.SMEM((4, 12), jnp.int32),
            pltpu.VMEM((BLOCKS, 128), jnp.int32),
            pltpu.VMEM((BLOCKS, 128), jnp.int32),
            pltpu.VMEM((BLOCKS, 128), F32),
            pltpu.VMEM((1, BLOCKS), jnp.int32),
            pltpu.VMEM((1, width), F32),
            block,
            block,
            pltpu.VMEM((2, width, rows), BF16),
            pltpu.VMEM((CHIPS, rows, 256), BF16),
            pltpu.VMEM((CHIPS, rows, 256), BF16),
            pltpu.VMEM((BLOCKS, 128), F32),
            pltpu.VMEM((width, rows), F32),
            block,
            pltpu.VMEM((2, width, rows), BF16),
            pltpu.VMEM((2, width, rows), BF16),
            lists,
            lists,
            lists,
            lists,
            pltpu.VMEM((HIDS, width, 128), BF16),
            pltpu.VMEM((HIDS, width, 128), BF16),
            pltpu.VMEM((width, HIDS * width), BF16),
            pltpu.VMEM((HIDS, width, rows), BF16),
            pltpu.VMEM((6, 8, 128), F32),
            pltpu.VMEM((5, 8, 128), F32),
            pltpu.VMEM((BLOCKS, 8, 128), F32),
            pltpu.VMEM((BLOCKS, 8, 128), F32),
            pltpu.VMEM((8, 128), F32),
            pltpu.VMEM((BLOCKS, 8, 128), F32),
            dma((10,)),
            dma((2, CHIPS, 2)),
            dma((2, CHIPS, 2)),
            dma((2,)),
            dma((2,)),
            dma((2, CHIPS, 2)),
            dma((2, CHIPS, 2)),
            dma((2,)),
            dma((2,)),
            dma((HIDS,)),
            dma((HIDS,)),
            dma((5,)),
            dma((5,)),
            dma((2, HIDS)),
            dma((2, HIDS)),
            dma((BLOCKS,)),
            dma((BLOCKS,)),
            dma((BLOCKS,)),
            dma((BLOCKS,)),
        ],
        compiler_params=pltpu.CompilerParams(
            collective_id=0, has_side_effects=True, vmem_limit_bytes=56 << 20
        ),
    )(
        weight.T,
        features,
        band_tiles,
        tile_live.T,
        send_rows[0],
        recv_rows[0],
        edge_weight[0],
        live_slots,
        bias_terms.reshape(1, width),
        cotangent,
    )
    output, feature_grad, wg, bg = pl.pallas_call(
        finish,
        out_shape=tuple(jax.ShapeDtypeStruct(*r) for r in results),
        in_specs=[vmem] * 4,
        out_specs=(hbm,) * 4,
        scratch_shapes=[dma((4,))],
        compiler_params=pltpu.CompilerParams(vmem_limit_bytes=4 << 20),
    )(*parts)
    return (output, feature_grad, wg.T, bg.reshape(width))


def solution(mesh):
    return jax.shard_map(
        on_device,
        mesh=mesh,
        in_specs=(
            P(None, "dom"),
            P(None, "hid"),
            P(None, "dom"),
            P(None, "dom"),
            P("dom", None, None),
            P("dom", None, None),
            P("dom", None, None),
            P("dom", None),
            P("hid"),
            P("hid", "dom"),
        ),
        out_specs=(P("hid", "dom"), P("hid", "dom"), P(None, "hid"), P("hid")),
        check_vma=False,
    )
```

```python
import jax
import jax.numpy as jnp
from jax import lax
from jax.experimental import pallas as pl
from jax.experimental.pallas import tpu as pltpu
from jax.sharding import PartitionSpec as P

MESH = pl.DeviceIdType.MESH
F32 = jnp.float32
BF16 = jnp.bfloat16
TILE = 256
NT = (((1,), (1,)), ((), ()))
ZS = 8
LISTS = 4
BLOCKS = 32
HIDS = 8


def dot(a, b):
    return jnp.dot(a, b, preferred_element_type=F32)


def dot_nt(a, b):
    return lax.dot_general(a, b, NT, preferred_element_type=F32)


def row_to_column(row, rows):
    lanes = row.shape[1]
    at = lax.broadcasted_iota(jnp.int32, (rows, lanes), 0)
    to = lax.broadcasted_iota(jnp.int32, (rows, lanes), 1)
    return jnp.sum(jnp.where(at == to, row, 0.0), axis=1, keepdims=True)


def kernel(
    wt_hbm,
    feat_hbm,
    band_hbm,
    live_hbm,
    send_hbm,
    recv_hbm,
    ew_hbm,
    slots_hbm,
    bias_hbm,
    cot_hbm,
    out_ref,
    fg_ref,
    wg_ref,
    bg_ref,
    wt_ref,
    feat,
    band,
    live_ref,
    send_ref,
    recv_ref,
    ew_ref,
    slots_ref,
    bias_ref,
    cot,
    mapped,
    mapped_tiles,
    near,
    picks,
    puts,
    weights,
    acc,
    sparse,
    pre,
    pre_tiles,
    term,
    term_in,
    out1,
    in1,
    out2,
    in2,
    wsend,
    wrecv,
    wfull,
    gb,
    bias_out,
    bias_in,
    pieces,
    pieces_in,
    summed,
    wg_all,
    load_sem,
    a1_send,
    a1_recv,
    n1_send,
    n1_recv,
    a2_send,
    a2_recv,
    n2_send,
    n2_recv,
    w_send,
    w_recv,
    b_send,
    b_recv,
    g_send,
    g_recv,
    rs_send,
    rs_recv,
    ag_send,
    ag_recv,
):
    me = lax.axis_index("dom")
    hid = lax.axis_index("hid")
    core = lax.rem(me, 2)
    z = lax.rem(me // 2, ZS)
    yh = me // (2 * ZS)
    left = lax.rem(me + BLOCKS - 1, BLOCKS)
    right = lax.rem(me + 1, BLOCKS)
    rows = mapped.shape[1]
    width = mapped.shape[0]
    half = width // 2
    barrier = pltpu.get_barrier_semaphore()

    @pl.loop(1, BLOCKS)
    def _(j):
        pl.semaphore_signal(barrier, inc=1, device_id={"dom": lax.rem(me + j, BLOCKS)}, device_id_type=MESH)

    @pl.loop(1, HIDS)
    def _(j):
        pl.semaphore_signal(barrier, inc=1, device_id={"hid": lax.rem(hid + j, HIDS)}, device_id_type=MESH)

    loads = [
        pltpu.make_async_copy(src, dst, load_sem.at[i])
        for i, (src, dst) in enumerate((
            (wt_hbm, wt_ref), (feat_hbm, feat), (send_hbm, send_ref), (slots_hbm, slots_ref),
            (ew_hbm, ew_ref), (recv_hbm, recv_ref), (bias_hbm, bias_ref), (live_hbm, live_ref),
            (band_hbm, band), (cot_hbm, cot),
        ))
    ]
    for load in loads:
        load.start()

    def remote(src, dst, ssem, rsem, **where):
        return pltpu.make_async_remote_copy(
            src_ref=src, dst_ref=dst, send_sem=ssem, recv_sem=rsem,
            device_id=where, device_id_type=MESH,
        )

    def offset(step):
        far = (step + 1) // 2
        return lax.rem(4 + far * (1 - 2 * lax.rem(step, 2)) + ZS, ZS)

    def chip_at(dz, dy):
        return lax.rem(yh + dy, 2) * ZS + lax.rem(z + dz, ZS)

    def list_row(ref, dz):
        return jnp.concatenate(
            [ref[pl.ds(2 * chip_at(dz, dy) + c, 1), :] for dy in range(2) for c in range(2)], axis=1
        )

    def onehot(index):
        at = lax.broadcasted_iota(jnp.int32, (TILE, LISTS * 128), 0)
        return jnp.where(at == index % TILE, 1.0, 0.0).astype(BF16)

    def from_tiles(stacked, index):
        tile = index // TILE
        height = stacked.shape[0] // 4
        got = stacked[3 * height:]
        for t in range(3):
            got = jnp.where(tile == t, stacked[t * height:(t + 1) * height], got)
        return got

    def to_tiles(values, index):
        tile = index // TILE
        return jnp.concatenate(
            [jnp.where(tile == t, values, 0.0).astype(BF16) for t in range(4)], axis=0
        )

    def side_by_side(stacked):
        height = stacked.shape[0] // 4
        return jnp.concatenate([stacked[t * height:(t + 1) * height] for t in range(4)], axis=1)

    for load in loads[:4]:
        load.wait()

    @pl.loop(0, rows // TILE)
    def _(j):
        cols = pl.ds(pl.multiple_of(j * TILE, TILE), TILE)
        got = dot(wt_ref[...], feat[:, cols]).astype(BF16)
        mapped[:, cols] = got
        mapped_tiles[pl.ds(pl.multiple_of(j * width, width), width), :] = got

    pl.semaphore_wait(barrier, BLOCKS - 1 + HIDS - 1)

    to_right = remote(mapped, near.at[0], n1_send.at[0], n1_recv.at[0], dom=right)
    to_left = remote(mapped, near.at[1], n1_send.at[1], n1_recv.at[1], dom=left)
    to_right.start()
    to_left.start()

    def pick(dz):
        index = list_row(send_ref, dz)
        picks[dz] = onehot(index)
        got = from_tiles(dot(mapped_tiles[...], picks[dz]), index).astype(BF16)
        for h in range(2):
            for i in range(LISTS):
                out1[h, dz, i] = got[h * half:(h + 1) * half, i * 128:(i + 1) * 128]

    def buffers(first):
        return (out1, in1, a1_send, a1_recv) if first else (out2, in2, a2_send, a2_recv)

    def ship(first, h, dz, dy, c):
        outs, ins, ssem, rsem = buffers(first)
        back = lax.rem(ZS - dz, ZS)
        return remote(
            outs.at[h, dz, 2 * dy + c], ins.at[h, back, 2 * dy + core],
            ssem.at[h, dz, 2 * dy + c], rsem.at[h, back, 2 * dy + core],
            dom=2 * chip_at(dz, dy) + c,
        )

    def ship_four(first, h, dz):
        for dy in (1, 0):
            for c in range(2):
                ship(first, h, dz, dy, c).start()

    def ship_near(first, h):
        outs, ins, _, _ = buffers(first)
        for c in range(2):
            ship(first, h, 0, 1, c).start()
        ship(first, h, 0, 0, 1 - core).start()
        ins[h, 0, core] = outs[h, 0, core]

    def arrive(first, h, dz, i):
        outs, ins, ssem, rsem = buffers(first)
        remote(outs.at[h, dz, i], ins.at[h, dz, i], ssem.at[h, dz, i], rsem.at[h, dz, i], dom=left).wait_recv()

    def arrive_four(first, h, dz):
        for i in (2, 3, 0, 1):
            arrive(first, h, dz, i)

    def arrive_near(first, h):
        for i in (2, 3, 1 - core):
            arrive(first, h, 0, i)

    @pl.loop(0, ZS - 1)
    def _(step):
        dz = offset(step)
        pick(dz)
        ship_four(True, 0, dz)

    pick(0)
    ship_near(True, 0)

    @pl.loop(0, ZS - 1)
    def _(step):
        ship_four(True, 1, offset(step))

    ship_near(True, 1)

    for load in loads[4:]:
        load.wait()

    wt = wt_ref[...]
    wsend[...] = jnp.zeros_like(wsend)
    for p in range(HIDS):
        wsend[p, :, :width] = wt[:, p * width:(p + 1) * width]
    wrecv[0] = wsend[hid]

    @pl.loop(1, HIDS)
    def _(j):
        peer = lax.rem(hid + j, HIDS)
        remote(wsend.at[peer], wrecv.at[HIDS - j], w_send.at[j], w_recv.at[HIDS - j], hid=peer).start()

    slot_ids = lax.broadcasted_iota(jnp.int32, (BLOCKS, 128), 1).astype(F32)
    counts = row_to_column(slots_ref[...].astype(F32), BLOCKS)
    weights[...] = jnp.where(slot_ids < counts, ew_ref[...], 0.0)

    def dense_forward(source, s):
        @pl.loop(0, rows // TILE)
        def _(j):
            cols = pl.ds(pl.multiple_of(j * TILE, TILE), TILE)
            parts = [
                (source[:, t * TILE:(t + 1) * TILE].astype(F32)
                 * live_ref[j, s * 4 + t].astype(F32)).astype(BF16)
                for t in range(rows // TILE)
            ]
            got = dot(jnp.concatenate(parts, axis=1), band[s * rows:(s + 1) * rows, cols])
            if s == 1:
                acc[:, cols] = got
            else:
                acc[:, cols] += got

    dense_forward(mapped, 1)

    @pl.loop(0, ZS)
    def _(dz):
        puts[dz] = onehot(list_row(recv_ref, dz))

    to_right.wait_recv()
    dense_forward(near.at[0], 0)
    to_left.wait_recv()
    dense_forward(near.at[1], 2)

    bias_in_col = row_to_column(bias_ref[...], width)

    def lists_in(ins, h, dz):
        return jnp.concatenate([ins[h, dz, i] for i in range(LISTS)], axis=1).astype(F32)

    def put(h, dz):
        values = lists_in(in1, h, dz) * list_row(weights, dz)
        sparse[h] += dot_nt(to_tiles(values, list_row(recv_ref, dz)), puts[dz])

    def activate(h):
        part = slice(h * half, (h + 1) * half)
        sparse[h] = jnp.zeros_like(sparse[h])

        @pl.loop(0, ZS - 1)
        def _(step):
            dz = offset(step)
            arrive_four(True, h, dz)
            put(h, dz)

        arrive_near(True, h)
        put(h, 0)
        act = acc[part] + bias_in_col[part] + side_by_side(sparse[h])
        gate = 1.0 / (1.0 + jnp.exp(-act))
        out_ref[part] = (act * gate).astype(BF16)
        grad = (cot[part].astype(F32) * (gate * (1.0 + act * (1.0 - gate)))).astype(BF16)
        pre[part] = grad
        for t in range(4):
            pre_tiles[h, t * half:(t + 1) * half] = grad[:, t * TILE:(t + 1) * TILE]

    def message(h, dz):
        got = from_tiles(dot(pre_tiles[h], puts[dz]), list_row(recv_ref, dz))
        got = (got * list_row(weights, dz)).astype(BF16)
        for i in range(LISTS):
            out2[h, dz, i] = got[:, i * 128:(i + 1) * 128]

    def send_messages(h):
        @pl.loop(0, ZS - 1)
        def _(step):
            dz = offset(step)
            message(h, dz)
            ship_four(False, h, dz)

        message(h, 0)
        ship_near(False, h)

    def dense_backward(target, s):
        @pl.loop(0, rows // TILE)
        def _(t):
            cols = pl.ds(pl.multiple_of(t * TILE, TILE), TILE)
            parts = [
                (pre[:, j * TILE:(j + 1) * TILE].astype(F32)
                 * live_ref[j, s * 4 + t].astype(F32)).astype(BF16)
                for j in range(rows // TILE)
            ]
            band_rows = pl.ds(pl.multiple_of(s * rows + t * TILE, TILE), TILE)
            got = dot_nt(jnp.concatenate(parts, axis=1), band[band_rows, :])
            target[:, cols] = got.astype(target.dtype)

    def bias_copy(step):
        bit = 1 << step
        peer = me + bit * (1 - 2 * lax.rem(me // bit, 2))
        return remote(bias_out.at[step], bias_in.at[step], b_send.at[step], b_recv.at[step], dom=peer)

    def bias_step(step):
        bias_copy(step).wait_recv()
        bias_out[step + 1] = bias_out[step] + bias_in[step]
        if step < 4:
            bias_copy(step + 1).start()

    activate(0)
    send_messages(0)
    activate(1)

    dense_backward(term.at[0], 0)
    grad_left = remote(term.at[0], term_in.at[0], n2_send.at[0], n2_recv.at[0], dom=left)
    grad_left.start()
    dense_backward(term.at[1], 2)
    grad_right = remote(term.at[1], term_in.at[1], n2_send.at[1], n2_recv.at[1], dom=right)
    grad_right.start()
    bias_col = jnp.sum(pre[...].astype(F32), axis=1, keepdims=True)
    diagonal = lax.broadcasted_iota(jnp.int32, (width, 128), 0) == lax.broadcasted_iota(jnp.int32, (width, 128), 1)
    bias_row = jnp.sum(jnp.where(diagonal, bias_col, 0.0), axis=0, keepdims=True)
    bias_out[0] = jnp.broadcast_to(bias_row, (8, 128))
    bias_copy(0).start()
    send_messages(1)
    bias_step(0)

    dense_backward(acc, 1)

    @pl.loop(1, HIDS)
    def _(j):
        remote(wsend.at[j], wrecv.at[j], w_send.at[j], w_recv.at[j], dom=left).wait_recv()

    wfull[...] = jnp.transpose(
        wrecv[...].reshape(HIDS * width, 128).astype(F32), (1, 0)
    )[:width].astype(BF16)

    grad_left.wait_recv()
    grad_right.wait_recv()
    acc[...] += term_in[0].astype(F32) + term_in[1].astype(F32)

    def give_back(h, dz):
        sparse[h] += dot_nt(to_tiles(lists_in(in2, h, dz), list_row(send_ref, dz)), picks[dz])

    def gradient(h):
        part = slice(h * half, (h + 1) * half)
        sparse[h] = jnp.zeros_like(sparse[h])

        @pl.loop(0, ZS - 1)
        def _(step):
            dz = offset(step)
            arrive_four(False, h, dz)
            give_back(h, dz)

        arrive_near(False, h)
        give_back(h, 0)
        gb[0, part] = (acc[part] + side_by_side(sparse[h])).astype(BF16)

    def share(h, j):
        part = pl.ds(h * half, half)
        return remote(
            gb.at[0, part], gb.at[HIDS - j, part], g_send.at[h, j], g_recv.at[h, HIDS - j],
            hid=lax.rem(hid + j, HIDS),
        )

    def share_all(h):
        @pl.loop(1, HIDS)
        def _(j):
            share(h, j).start()

    gradient(0)
    share_all(0)
    gradient(1)

    wg = dot_nt(gb[0], feat[...])
    for d in range(BLOCKS):
        r, c = d // 4, d % 4
        pieces[d] = wg[8 * r:8 * r + 8, 128 * c:128 * c + 128]

    @pl.loop(1, BLOCKS)
    def _(j):
        peer = lax.rem(me + j, BLOCKS)
        remote(pieces.at[peer], pieces_in.at[BLOCKS - j], rs_send.at[j], rs_recv.at[BLOCKS - j], dom=peer).start()

    share_all(1)
    bias_step(1)
    summed[...] = pieces[me]

    @pl.loop(1, BLOCKS)
    def _(j):
        remote(pieces.at[j], pieces_in.at[j], rs_send.at[j], rs_recv.at[j], dom=left).wait_recv()
        summed[...] += pieces_in[j]

    @pl.loop(1, BLOCKS)
    def _(j):
        peer = lax.rem(me + j, BLOCKS)
        remote(summed, wg_all.at[me], ag_send.at[j], ag_recv.at[BLOCKS - j], dom=peer).start()

    wg_all[me] = summed[...]
    bias_step(2)
    bias_step(3)

    for h in range(2):
        @pl.loop(1, HIDS)
        def _(j):
            part = pl.ds(h * half, half)
            remote(gb.at[0, part], gb.at[j, part], g_send.at[h, j], g_recv.at[h, j], dom=left).wait_recv()

    @pl.loop(0, rows // TILE)
    def _(j):
        cols = pl.ds(pl.multiple_of(j * TILE, TILE), TILE)
        stack = gb[:, :, cols].reshape(HIDS * width, TILE)
        fg_ref[:, cols] = dot(wfull[...], stack).astype(BF16)

    bias_step(4)
    bg_ref[...] = bias_out[5, 0:1, :width]

    @pl.loop(1, BLOCKS)
    def _(j):
        remote(summed, wg_all.at[lax.rem(me + j, BLOCKS)], ag_send.at[j], ag_recv.at[j], dom=left).wait_recv()

    for d in range(BLOCKS):
        r, c = d // 4, d % 4
        wg_ref[8 * r:8 * r + 8, 128 * c:128 * c + 128] = wg_all[d]

    to_right.wait_send()
    to_left.wait_send()
    grad_left.wait_send()
    grad_right.wait_send()
    for step in range(5):
        bias_copy(step).wait_send()

    @pl.loop(1, ZS)
    def _(dz):
        for first in (True, False):
            for h in range(2):
                for dy in range(2):
                    for c in range(2):
                        ship(first, h, dz, dy, c).wait_send()

    for first in (True, False):
        for h in range(2):
            for c in range(2):
                ship(first, h, 0, 1, c).wait_send()
            ship(first, h, 0, 0, 1 - core).wait_send()

    @pl.loop(1, HIDS)
    def _(j):
        peer = lax.rem(hid + j, HIDS)
        remote(wsend.at[peer], wrecv.at[HIDS - j], w_send.at[j], w_recv.at[HIDS - j], hid=peer).wait_send()
        for h in range(2):
            share(h, j).wait_send()

    @pl.loop(1, BLOCKS)
    def _(j):
        peer = lax.rem(me + j, BLOCKS)
        remote(pieces.at[peer], pieces_in.at[BLOCKS - j], rs_send.at[j], rs_recv.at[BLOCKS - j], dom=peer).wait_send()
        remote(summed, wg_all.at[me], ag_send.at[j], ag_recv.at[BLOCKS - j], dom=peer).wait_send()


def finish(*refs):
    sources, targets, sem = refs[:4], refs[4:8], refs[8]
    copies = [
        pltpu.make_async_copy(src, dst, sem.at[i])
        for i, (src, dst) in enumerate(zip(sources, targets))
    ]
    for copy in copies:
        copy.start()
    for copy in copies:
        copy.wait()


def on_device(
    features,
    weight,
    band_tiles,
    tile_live,
    send_rows,
    recv_rows,
    edge_weight,
    live_slots,
    bias_terms,
    cotangent,
):
    depth, rows = features.shape
    width = weight.shape[1]
    vmem = pl.BlockSpec(memory_space=pltpu.VMEM)
    hbm = pl.BlockSpec(memory_space=pltpu.HBM)
    dma = pltpu.SemaphoreType.DMA
    block = pltpu.VMEM((width, rows), BF16)
    lists = pltpu.VMEM((2, ZS, LISTS, width // 2, 128), BF16)
    results = (((width, rows), BF16), ((width, rows), BF16), ((width, depth), F32), ((1, width), F32))
    parts = pl.pallas_call(
        kernel,
        out_shape=tuple(pltpu.VMEM(*r) for r in results),
        in_specs=[hbm] * 10,
        out_specs=(vmem,) * 4,
        scratch_shapes=[
            pltpu.VMEM((width, depth), BF16),
            pltpu.VMEM((depth, rows), BF16),
            pltpu.VMEM((3 * rows, rows), BF16),
            pltpu.SMEM((4, 12), jnp.int32),
            pltpu.VMEM((BLOCKS, 128), jnp.int32),
            pltpu.VMEM((BLOCKS, 128), jnp.int32),
            pltpu.VMEM((BLOCKS, 128), F32),
            pltpu.VMEM((1, BLOCKS), jnp.int32),
            pltpu.VMEM((1, width), F32),
            block,
            block,
            pltpu.VMEM((4 * width, TILE), BF16),
            pltpu.VMEM((2, width, rows), BF16),
            pltpu.VMEM((ZS, TILE, LISTS * 128), BF16),
            pltpu.VMEM((ZS, TILE, LISTS * 128), BF16),
            pltpu.VMEM((BLOCKS, 128), F32),
            pltpu.VMEM((width, rows), F32),
            pltpu.VMEM((2, 2 * width, TILE), F32),
            block,
            pltpu.VMEM((2, 2 * width, TILE), BF16),
            pltpu.VMEM((2, width, rows), BF16),
            pltpu.VMEM((2, width, rows), BF16),
            lists,
            lists,
            lists,
            lists,
            pltpu.VMEM((HIDS, width, 128), BF16),
            pltpu.VMEM((HIDS, width, 128), BF16),
            pltpu.VMEM((width, HIDS * width), BF16),
            pltpu.VMEM((HIDS, width, rows), BF16),
            pltpu.VMEM((6, 8, 128), F32),
            pltpu.VMEM((5, 8, 128), F32),
            pltpu.VMEM((BLOCKS, 8, 128), F32),
            pltpu.VMEM((BLOCKS, 8, 128), F32),
            pltpu.VMEM((8, 128), F32),
            pltpu.VMEM((BLOCKS, 8, 128), F32),
            dma((10,)),
            dma((2, ZS, LISTS)),
            dma((2, ZS, LISTS)),
            dma((2,)),
            dma((2,)),
            dma((2, ZS, LISTS)),
            dma((2, ZS, LISTS)),
            dma((2,)),
            dma((2,)),
            dma((HIDS,)),
            dma((HIDS,)),
            dma((5,)),
            dma((5,)),
            dma((2, HIDS)),
            dma((2, HIDS)),
            dma((BLOCKS,)),
            dma((BLOCKS,)),
            dma((BLOCKS,)),
            dma((BLOCKS,)),
        ],
        compiler_params=pltpu.CompilerParams(
            collective_id=0, has_side_effects=True, vmem_limit_bytes=56 << 20
        ),
    )(
        weight.T,
        features,
        band_tiles,
        tile_live.T,
        send_rows[0],
        recv_rows[0],
        edge_weight[0],
        live_slots,
        bias_terms.reshape(1, width),
        cotangent,
    )
    output, feature_grad, wg, bg = pl.pallas_call(
        finish,
        out_shape=tuple(jax.ShapeDtypeStruct(*r) for r in results),
        in_specs=[vmem] * 4,
        out_specs=(hbm,) * 4,
        scratch_shapes=[dma((4,))],
        compiler_params=pltpu.CompilerParams(vmem_limit_bytes=4 << 20),
    )(*parts)
    return (output, feature_grad, wg.T, bg.reshape(width))


def solution(mesh):
    return jax.shard_map(
        on_device,
        mesh=mesh,
        in_specs=(
            P(None, "dom"),
            P(None, "hid"),
            P(None, "dom"),
            P(None, "dom"),
            P("dom", None, None),
            P("dom", None, None),
            P("dom", None, None),
            P("dom", None),
            P("hid"),
            P("hid", "dom"),
        ),
        out_specs=(P("hid", "dom"), P("hid", "dom"), P(None, "hid"), P("hid")),
        check_vma=False,
    )
```

```python
import jax
import jax.numpy as jnp
from jax import lax
from jax.experimental import pallas as pl
from jax.experimental.pallas import tpu as pltpu
from jax.sharding import PartitionSpec as P

MESH = pl.DeviceIdType.MESH
F32 = jnp.float32
BF16 = jnp.bfloat16
TILE = 256
NT = (((1,), (1,)), ((), ()))
ZS = 8
LISTS = 4
BLOCKS = 32
HIDS = 8


def dot(a, b):
    return jnp.dot(a, b, preferred_element_type=F32)


def dot_nt(a, b):
    return lax.dot_general(a, b, NT, preferred_element_type=F32)


def row_to_column(row, rows):
    lanes = row.shape[1]
    at = lax.broadcasted_iota(jnp.int32, (rows, lanes), 0)
    to = lax.broadcasted_iota(jnp.int32, (rows, lanes), 1)
    return jnp.sum(jnp.where(at == to, row, 0.0), axis=1, keepdims=True)


def kernel(
    wt_hbm,
    feat_hbm,
    band_hbm,
    live_hbm,
    send_hbm,
    recv_hbm,
    ew_hbm,
    slots_hbm,
    bias_hbm,
    cot_hbm,
    out_ref,
    fg_ref,
    wg_ref,
    bg_ref,
    wt_ref,
    feat,
    band,
    live_ref,
    send_ref,
    recv_ref,
    ew_ref,
    slots_ref,
    bias_ref,
    cot,
    mapped,
    mapped_tiles,
    near,
    picks,
    puts,
    weights,
    acc,
    sparse,
    pre,
    pre_tiles,
    term,
    term_in,
    out1,
    in1,
    out2,
    in2,
    wsend,
    wrecv,
    wfull,
    gb,
    bias_out,
    bias_in,
    pieces,
    pieces_in,
    summed,
    wg_all,
    load_sem,
    a1_send,
    a1_recv,
    n1_send,
    n1_recv,
    a2_send,
    a2_recv,
    n2_send,
    n2_recv,
    w_send,
    w_recv,
    b_send,
    b_recv,
    g_send,
    g_recv,
    rs_send,
    rs_recv,
    ag_send,
    ag_recv,
):
    me = lax.axis_index("dom")
    hid = lax.axis_index("hid")
    core = lax.rem(me, 2)
    z = lax.rem(me // 2, ZS)
    yh = me // (2 * ZS)
    left = lax.rem(me + BLOCKS - 1, BLOCKS)
    right = lax.rem(me + 1, BLOCKS)
    rows = mapped.shape[1]
    width = mapped.shape[0]
    half = width // 2
    barrier = pltpu.get_barrier_semaphore()

    @pl.loop(1, BLOCKS)
    def _(j):
        pl.semaphore_signal(barrier, inc=1, device_id={"dom": lax.rem(me + j, BLOCKS)}, device_id_type=MESH)

    @pl.loop(1, HIDS)
    def _(j):
        pl.semaphore_signal(barrier, inc=1, device_id={"hid": lax.rem(hid + j, HIDS)}, device_id_type=MESH)

    loads = [
        pltpu.make_async_copy(src, dst, load_sem.at[i])
        for i, (src, dst) in enumerate((
            (wt_hbm, wt_ref), (feat_hbm, feat), (send_hbm, send_ref), (slots_hbm, slots_ref),
            (ew_hbm, ew_ref), (recv_hbm, recv_ref), (bias_hbm, bias_ref), (live_hbm, live_ref),
            (band_hbm, band), (cot_hbm, cot),
        ))
    ]
    for load in loads:
        load.start()

    def remote(src, dst, ssem, rsem, **where):
        return pltpu.make_async_remote_copy(
            src_ref=src, dst_ref=dst, send_sem=ssem, recv_sem=rsem,
            device_id=where, device_id_type=MESH,
        )

    def offset(step):
        far = (step + 1) // 2
        return lax.rem(4 + far * (1 - 2 * lax.rem(step, 2)) + ZS, ZS)

    def chip_at(dz, dy):
        return lax.rem(yh + dy, 2) * ZS + lax.rem(z + dz, ZS)

    def list_row(ref, dz):
        return jnp.concatenate(
            [ref[pl.ds(2 * chip_at(dz, dy) + c, 1), :] for dy in range(2) for c in range(2)], axis=1
        )

    def onehot(index):
        at = lax.broadcasted_iota(jnp.int32, (TILE, LISTS * 128), 0)
        return jnp.where(at == index % TILE, 1.0, 0.0).astype(BF16)

    def from_tiles(stacked, index):
        tile = index // TILE
        height = stacked.shape[0] // 4
        got = stacked[3 * height:]
        for t in range(3):
            got = jnp.where(tile == t, stacked[t * height:(t + 1) * height], got)
        return got

    def to_tiles(values, index):
        tile = index // TILE
        return jnp.concatenate(
            [jnp.where(tile == t, values, 0.0).astype(BF16) for t in range(4)], axis=0
        )

    def side_by_side(stacked):
        height = stacked.shape[0] // 4
        return jnp.concatenate([stacked[t * height:(t + 1) * height] for t in range(4)], axis=1)

    for load in loads[:4]:
        load.wait()

    @pl.loop(0, rows // TILE)
    def _(j):
        cols = pl.ds(pl.multiple_of(j * TILE, TILE), TILE)
        got = dot(wt_ref[...], feat[:, cols]).astype(BF16)
        mapped[:, cols] = got
        mapped_tiles[pl.ds(pl.multiple_of(j * width, width), width), :] = got

    pl.semaphore_wait(barrier, BLOCKS - 1 + HIDS - 1)

    to_right = remote(mapped, near.at[0], n1_send.at[0], n1_recv.at[0], dom=right)
    to_left = remote(mapped, near.at[1], n1_send.at[1], n1_recv.at[1], dom=left)
    to_right.start()
    to_left.start()

    def pick(dz):
        index = list_row(send_ref, dz)
        picks[dz] = onehot(index)
        got = from_tiles(dot(mapped_tiles[...], picks[dz]), index).astype(BF16)
        for h in range(2):
            for i in range(LISTS):
                out1[h, LISTS * dz + i] = got[h * half:(h + 1) * half, i * 128:(i + 1) * 128]

    def buffers(first):
        return (out1, in1, a1_send, a1_recv) if first else (out2, in2, a2_send, a2_recv)

    def ship(first, h, dz, dy, c):
        outs, ins, ssem, rsem = buffers(first)
        back = lax.rem(ZS - dz, ZS)
        return remote(
            outs.at[h, LISTS * dz + 2 * dy + c], ins.at[h, LISTS * back + 2 * dy + core],
            ssem.at[h], rsem.at[h, back], dom=2 * chip_at(dz, dy) + c,
        )

    def sent(first, h):
        outs, ins, ssem, rsem = buffers(first)
        every = pl.ds(1, BLOCKS - 1)
        remote(outs.at[h, every], ins.at[h, every], ssem.at[h], rsem.at[h, 0], dom=left).wait_send()

    def ship_four(first, h, dz):
        for dy in (1, 0):
            for c in range(2):
                ship(first, h, dz, dy, c).start()

    def ship_near(first, h):
        outs, ins, _, _ = buffers(first)
        for c in range(2):
            ship(first, h, 0, 1, c).start()
        ship(first, h, 0, 0, 1 - core).start()
        ins[h, core] = outs[h, core]

    def arrive(first, h, dz, count):
        outs, ins, ssem, rsem = buffers(first)
        these = pl.ds(LISTS * dz, count)
        remote(outs.at[h, these], ins.at[h, these], ssem.at[h], rsem.at[h, dz], dom=left).wait_recv()

    def arrive_four(first, h, dz):
        arrive(first, h, dz, LISTS)

    def arrive_near(first, h):
        arrive(first, h, 0, LISTS - 1)

    @pl.loop(0, ZS - 1)
    def _(step):
        dz = offset(step)
        pick(dz)
        ship_four(True, 0, dz)

    pick(0)
    ship_near(True, 0)

    @pl.loop(0, ZS - 1)
    def _(step):
        ship_four(True, 1, offset(step))

    ship_near(True, 1)

    for load in loads[4:]:
        load.wait()

    wt = wt_ref[...]
    wsend[...] = jnp.zeros_like(wsend)
    for p in range(HIDS):
        wsend[p, :, :width] = wt[:, p * width:(p + 1) * width]
    wrecv[0] = wsend[hid]

    @pl.loop(1, HIDS)
    def _(j):
        peer = lax.rem(hid + j, HIDS)
        remote(wsend.at[peer], wrecv.at[HIDS - j], w_send.at[0], w_recv.at[0], hid=peer).start()

    slot_ids = lax.broadcasted_iota(jnp.int32, (BLOCKS, 128), 1).astype(F32)
    counts = row_to_column(slots_ref[...].astype(F32), BLOCKS)
    weights[...] = jnp.where(slot_ids < counts, ew_ref[...], 0.0)

    def dense_forward(source, s):
        @pl.loop(0, rows // TILE)
        def _(j):
            cols = pl.ds(pl.multiple_of(j * TILE, TILE), TILE)
            parts = [
                (source[:, t * TILE:(t + 1) * TILE].astype(F32)
                 * live_ref[j, s * 4 + t].astype(F32)).astype(BF16)
                for t in range(rows // TILE)
            ]
            got = dot(jnp.concatenate(parts, axis=1), band[s * rows:(s + 1) * rows, cols])
            if s == 1:
                acc[:, cols] = got
            else:
                acc[:, cols] += got

    dense_forward(mapped, 1)

    @pl.loop(0, ZS)
    def _(dz):
        puts[dz] = onehot(list_row(recv_ref, dz))

    to_right.wait_recv()
    dense_forward(near.at[0], 0)
    to_left.wait_recv()
    dense_forward(near.at[1], 2)

    bias_in_col = row_to_column(bias_ref[...], width)

    def lists_in(ins, h, dz):
        return jnp.concatenate([ins[h, LISTS * dz + i] for i in range(LISTS)], axis=1).astype(F32)

    def put(h, dz):
        values = lists_in(in1, h, dz) * list_row(weights, dz)
        sparse[h] += dot_nt(to_tiles(values, list_row(recv_ref, dz)), puts[dz])

    def activate(h):
        part = slice(h * half, (h + 1) * half)
        sparse[h] = jnp.zeros_like(sparse[h])

        @pl.loop(0, ZS - 1)
        def _(step):
            dz = offset(step)
            arrive_four(True, h, dz)
            put(h, dz)

        arrive_near(True, h)
        put(h, 0)
        act = acc[part] + bias_in_col[part] + side_by_side(sparse[h])
        gate = 1.0 / (1.0 + jnp.exp(-act))
        out_ref[part] = (act * gate).astype(BF16)
        grad = (cot[part].astype(F32) * (gate * (1.0 + act * (1.0 - gate)))).astype(BF16)
        pre[part] = grad
        for t in range(4):
            pre_tiles[h, t * half:(t + 1) * half] = grad[:, t * TILE:(t + 1) * TILE]

    def message(h, dz):
        got = from_tiles(dot(pre_tiles[h], puts[dz]), list_row(recv_ref, dz))
        got = (got * list_row(weights, dz)).astype(BF16)
        for i in range(LISTS):
            out2[h, LISTS * dz + i] = got[:, i * 128:(i + 1) * 128]

    def send_messages(h):
        @pl.loop(0, ZS - 1)
        def _(step):
            dz = offset(step)
            message(h, dz)
            ship_four(False, h, dz)

        message(h, 0)
        ship_near(False, h)

    def dense_backward(target, s):
        @pl.loop(0, rows // TILE)
        def _(t):
            cols = pl.ds(pl.multiple_of(t * TILE, TILE), TILE)
            parts = [
                (pre[:, j * TILE:(j + 1) * TILE].astype(F32)
                 * live_ref[j, s * 4 + t].astype(F32)).astype(BF16)
                for j in range(rows // TILE)
            ]
            band_rows = pl.ds(pl.multiple_of(s * rows + t * TILE, TILE), TILE)
            got = dot_nt(jnp.concatenate(parts, axis=1), band[band_rows, :])
            target[:, cols] = got.astype(target.dtype)

    def bias_copy(step):
        bit = 1 << step
        peer = me + bit * (1 - 2 * lax.rem(me // bit, 2))
        return remote(bias_out.at[step], bias_in.at[step], b_send.at[step], b_recv.at[step], dom=peer)

    def bias_step(step):
        bias_copy(step).wait_recv()
        bias_out[step + 1] = bias_out[step] + bias_in[step]
        if step < 4:
            bias_copy(step + 1).start()

    activate(0)
    send_messages(0)
    activate(1)

    bias_col = jnp.sum(pre[...].astype(F32), axis=1, keepdims=True)
    diagonal = lax.broadcasted_iota(jnp.int32, (width, 128), 0) == lax.broadcasted_iota(jnp.int32, (width, 128), 1)
    bias_row = jnp.sum(jnp.where(diagonal, bias_col, 0.0), axis=0, keepdims=True)
    bias_out[0] = jnp.broadcast_to(bias_row, (8, 128))
    bias_copy(0).start()
    dense_backward(term.at[0], 0)
    grad_left = remote(term.at[0], term_in.at[0], n2_send.at[0], n2_recv.at[0], dom=left)
    grad_left.start()
    dense_backward(term.at[1], 2)
    grad_right = remote(term.at[1], term_in.at[1], n2_send.at[1], n2_recv.at[1], dom=right)
    grad_right.start()
    bias_step(0)
    send_messages(1)

    dense_backward(acc, 1)

    peers = pl.ds(1, HIDS - 1)
    slices = remote(wsend.at[peers], wrecv.at[peers], w_send.at[0], w_recv.at[0], dom=left)
    slices.wait_recv()
    slices.wait_send()

    wfull[...] = jnp.transpose(
        wrecv[...].reshape(HIDS * width, 128).astype(F32), (1, 0)
    )[:width].astype(BF16)

    grad_left.wait_recv()
    grad_right.wait_recv()
    acc[...] += term_in[0].astype(F32) + term_in[1].astype(F32)

    def give_back(h, dz):
        sparse[h] += dot_nt(to_tiles(lists_in(in2, h, dz), list_row(send_ref, dz)), picks[dz])

    def gradient(h):
        part = slice(h * half, (h + 1) * half)
        sparse[h] = jnp.zeros_like(sparse[h])

        @pl.loop(0, ZS - 1)
        def _(step):
            dz = offset(step)
            arrive_four(False, h, dz)
            give_back(h, dz)

        arrive_near(False, h)
        give_back(h, 0)
        gb[0, part] = (acc[part] + side_by_side(sparse[h])).astype(BF16)

    def share(h, j):
        part = pl.ds(h * half, half)
        return remote(
            gb.at[0, part], gb.at[HIDS - j, part], g_send.at[h], g_recv.at[h],
            hid=lax.rem(hid + j, HIDS),
        )

    def shared(h):
        part = pl.ds(h * half, half)
        return remote(gb.at[peers, part], gb.at[peers, part], g_send.at[h], g_recv.at[h], dom=left)

    def share_all(h):
        @pl.loop(1, HIDS)
        def _(j):
            share(h, j).start()

    bias_step(1)
    gradient(0)
    share_all(0)
    gradient(1)

    wg = dot_nt(gb[0], feat[...])
    for d in range(BLOCKS):
        r, c = d // 4, d % 4
        pieces[d] = wg[8 * r:8 * r + 8, 128 * c:128 * c + 128].astype(BF16)

    def reduce_piece(j):
        peer = lax.rem(me + j, BLOCKS)
        return remote(pieces.at[peer], pieces_in.at[BLOCKS - j], rs_send.at[0], rs_recv.at[0], dom=peer)

    def spread_piece(j):
        return remote(summed, wg_all.at[me], ag_send.at[0], ag_recv.at[0], dom=lax.rem(me + j, BLOCKS))

    @pl.loop(1, BLOCKS)
    def _(j):
        reduce_piece(j).start()

    share_all(1)
    bias_step(2)
    for h in range(2):
        sent(True, h)
        sent(False, h)

    pieces_in[0] = pieces[me]
    others = pl.ds(1, BLOCKS - 1)
    reduced = remote(pieces.at[others], pieces_in.at[others], rs_send.at[0], rs_recv.at[0], dom=left)
    reduced.wait_recv()
    summed[...] = jnp.sum(pieces_in[...].astype(F32), axis=0).astype(BF16)

    @pl.loop(1, BLOCKS)
    def _(j):
        spread_piece(j).start()

    wg_all[me] = summed[...]
    bias_step(3)
    reduced.wait_send()

    for h in range(2):
        shared(h).wait_recv()

    @pl.loop(0, rows // TILE)
    def _(j):
        cols = pl.ds(pl.multiple_of(j * TILE, TILE), TILE)
        stack = gb[:, :, cols].reshape(HIDS * width, TILE)
        fg_ref[:, cols] = dot(wfull[...], stack).astype(BF16)

    bias_step(4)
    bg_ref[...] = bias_out[5, 0:1, :width]

    spread = remote(pieces.at[others], wg_all.at[others], ag_send.at[0], ag_recv.at[0], dom=left)
    spread.wait_recv()

    for d in range(BLOCKS):
        r, c = d // 4, d % 4
        wg_ref[8 * r:8 * r + 8, 128 * c:128 * c + 128] = wg_all[d].astype(F32)

    to_right.wait_send()
    to_left.wait_send()
    grad_left.wait_send()
    grad_right.wait_send()
    for step in range(5):
        bias_copy(step).wait_send()

    for h in range(2):
        shared(h).wait_send()
    spread.wait_send()


def finish(*refs):
    sources, targets, sem = refs[:4], refs[4:8], refs[8]
    copies = [
        pltpu.make_async_copy(src, dst, sem.at[i])
        for i, (src, dst) in enumerate(zip(sources, targets))
    ]
    for copy in copies:
        copy.start()
    for copy in copies:
        copy.wait()


def on_device(
    features,
    weight,
    band_tiles,
    tile_live,
    send_rows,
    recv_rows,
    edge_weight,
    live_slots,
    bias_terms,
    cotangent,
):
    depth, rows = features.shape
    width = weight.shape[1]
    vmem = pl.BlockSpec(memory_space=pltpu.VMEM)
    hbm = pl.BlockSpec(memory_space=pltpu.HBM)
    dma = pltpu.SemaphoreType.DMA
    block = pltpu.VMEM((width, rows), BF16)
    lists = pltpu.VMEM((2, BLOCKS, width // 2, 128), BF16)
    results = (((width, rows), BF16), ((width, rows), BF16), ((width, depth), F32), ((1, width), F32))
    parts = pl.pallas_call(
        kernel,
        out_shape=tuple(pltpu.VMEM(*r) for r in results),
        in_specs=[hbm] * 10,
        out_specs=(vmem,) * 4,
        scratch_shapes=[
            pltpu.VMEM((width, depth), BF16),
            pltpu.VMEM((depth, rows), BF16),
            pltpu.VMEM((3 * rows, rows), BF16),
            pltpu.SMEM((4, 12), jnp.int32),
            pltpu.VMEM((BLOCKS, 128), jnp.int32),
            pltpu.VMEM((BLOCKS, 128), jnp.int32),
            pltpu.VMEM((BLOCKS, 128), F32),
            pltpu.VMEM((1, BLOCKS), jnp.int32),
            pltpu.VMEM((1, width), F32),
            block,
            block,
            pltpu.VMEM((4 * width, TILE), BF16),
            pltpu.VMEM((2, width, rows), BF16),
            pltpu.VMEM((ZS, TILE, LISTS * 128), BF16),
            pltpu.VMEM((ZS, TILE, LISTS * 128), BF16),
            pltpu.VMEM((BLOCKS, 128), F32),
            pltpu.VMEM((width, rows), F32),
            pltpu.VMEM((2, 2 * width, TILE), F32),
            block,
            pltpu.VMEM((2, 2 * width, TILE), BF16),
            pltpu.VMEM((2, width, rows), BF16),
            pltpu.VMEM((2, width, rows), BF16),
            lists,
            lists,
            lists,
            lists,
            pltpu.VMEM((HIDS, width, 128), BF16),
            pltpu.VMEM((HIDS, width, 128), BF16),
            pltpu.VMEM((width, HIDS * width), BF16),
            pltpu.VMEM((HIDS, width, rows), BF16),
            pltpu.VMEM((6, 8, 128), F32),
            pltpu.VMEM((5, 8, 128), F32),
            pltpu.VMEM((BLOCKS, 8, 128), BF16),
            pltpu.VMEM((BLOCKS, 8, 128), BF16),
            pltpu.VMEM((8, 128), BF16),
            pltpu.VMEM((BLOCKS, 8, 128), BF16),
            dma((10,)),
            dma((2,)),
            dma((2, ZS)),
            dma((2,)),
            dma((2,)),
            dma((2,)),
            dma((2, ZS)),
            dma((2,)),
            dma((2,)),
            dma((1,)),
            dma((1,)),
            dma((5,)),
            dma((5,)),
            dma((2,)),
            dma((2,)),
            dma((1,)),
            dma((1,)),
            dma((1,)),
            dma((1,)),
        ],
        compiler_params=pltpu.CompilerParams(
            collective_id=0, has_side_effects=True, vmem_limit_bytes=56 << 20
        ),
    )(
        weight.T,
        features,
        band_tiles,
        tile_live.T,
        send_rows[0],
        recv_rows[0],
        edge_weight[0],
        live_slots,
        bias_terms.reshape(1, width),
        cotangent,
    )
    output, feature_grad, wg, bg = pl.pallas_call(
        finish,
        out_shape=tuple(jax.ShapeDtypeStruct(*r) for r in results),
        in_specs=[vmem] * 4,
        out_specs=(hbm,) * 4,
        scratch_shapes=[dma((4,))],
        compiler_params=pltpu.CompilerParams(vmem_limit_bytes=4 << 20),
    )(*parts)
    return (output, feature_grad, wg.T, bg.reshape(width))


def solution(mesh):
    return jax.shard_map(
        on_device,
        mesh=mesh,
        in_specs=(
            P(None, "dom"),
            P(None, "hid"),
            P(None, "dom"),
            P(None, "dom"),
            P("dom", None, None),
            P("dom", None, None),
            P("dom", None, None),
            P("dom", None),
            P("hid"),
            P("hid", "dom"),
        ),
        out_specs=(P("hid", "dom"), P("hid", "dom"), P(None, "hid"), P("hid")),
        check_vma=False,
    )
```

```python
import jax
import jax.numpy as jnp
from jax import lax
from jax.experimental import pallas as pl
from jax.experimental.pallas import tpu as pltpu
from jax.sharding import PartitionSpec as P

MESH = pl.DeviceIdType.MESH
F32 = jnp.float32
BF16 = jnp.bfloat16
TILE = 256
NT = (((1,), (1,)), ((), ()))
ZS = 8
LISTS = 4
BLOCKS = 32
HIDS = 8
XS = 4


def dot(a, b):
    return jnp.dot(a, b, preferred_element_type=F32)


def dot_nt(a, b):
    return lax.dot_general(a, b, NT, preferred_element_type=F32)


def row_to_column(row, rows):
    lanes = row.shape[1]
    at = lax.broadcasted_iota(jnp.int32, (rows, lanes), 0)
    to = lax.broadcasted_iota(jnp.int32, (rows, lanes), 1)
    return jnp.sum(jnp.where(at == to, row, 0.0), axis=1, keepdims=True)


def kernel(
    wt_hbm,
    feat_hbm,
    band_hbm,
    live_hbm,
    send_hbm,
    recv_hbm,
    ew_hbm,
    slots_hbm,
    bias_hbm,
    cot_hbm,
    out_ref,
    fg_ref,
    wg_ref,
    bg_ref,
    wt_ref,
    feat,
    band,
    live_ref,
    send_ref,
    recv_ref,
    ew_ref,
    slots_ref,
    bias_ref,
    cot,
    mapped,
    mapped_tiles,
    near,
    picks,
    puts,
    weights,
    acc,
    sparse,
    pre,
    pre_tiles,
    term,
    term_in,
    out1,
    in1,
    out2,
    in2,
    wsend,
    wrecv,
    wfull,
    gb,
    bias_out,
    bias_in,
    pieces,
    pieces_in,
    summed,
    wg_all,
    load_sem,
    a1_send,
    a1_recv,
    n1_send,
    n1_recv,
    a2_send,
    a2_recv,
    n2_send,
    n2_recv,
    w_send,
    w_recv,
    b_send,
    b_recv,
    g_send,
    g_recv,
    rs_send,
    rs_recv,
    ag_send,
    ag_recv,
):
    me = lax.axis_index("dom")
    hid = lax.axis_index("hid")
    core = lax.rem(me, 2)
    z = lax.rem(me // 2, ZS)
    yh = me // (2 * ZS)
    left = lax.rem(me + BLOCKS - 1, BLOCKS)
    right = lax.rem(me + 1, BLOCKS)
    rows = mapped.shape[1]
    width = mapped.shape[0]
    half = width // 2
    barrier = pltpu.get_barrier_semaphore()

    @pl.loop(1, BLOCKS)
    def _(j):
        pl.semaphore_signal(barrier, inc=1, device_id={"dom": lax.rem(me + j, BLOCKS)}, device_id_type=MESH)

    @pl.loop(1, HIDS)
    def _(j):
        pl.semaphore_signal(barrier, inc=1, device_id={"hid": lax.rem(hid + j, HIDS)}, device_id_type=MESH)

    loads = [
        pltpu.make_async_copy(src, dst, load_sem.at[i])
        for i, (src, dst) in enumerate((
            (wt_hbm, wt_ref), (feat_hbm, feat), (send_hbm, send_ref), (slots_hbm, slots_ref),
            (ew_hbm, ew_ref), (recv_hbm, recv_ref), (bias_hbm, bias_ref), (live_hbm, live_ref),
            (band_hbm, band), (cot_hbm, cot),
        ))
    ]
    for load in loads:
        load.start()

    def remote(src, dst, ssem, rsem, **where):
        return pltpu.make_async_remote_copy(
            src_ref=src, dst_ref=dst, send_sem=ssem, recv_sem=rsem,
            device_id=where, device_id_type=MESH,
        )

    def offset(step):
        far = (step + 1) // 2
        return lax.rem(4 + far * (1 - 2 * lax.rem(step, 2)) + ZS, ZS)

    def chip_at(dz, dy):
        return lax.rem(yh + dy, 2) * ZS + lax.rem(z + dz, ZS)

    def list_row(ref, dz):
        return jnp.concatenate(
            [ref[pl.ds(2 * chip_at(dz, dy) + c, 1), :] for dy in range(2) for c in range(2)], axis=1
        )

    def onehot(index):
        at = lax.broadcasted_iota(jnp.int32, (TILE, LISTS * 128), 0)
        return jnp.where(at == index % TILE, 1.0, 0.0).astype(BF16)

    def from_tiles(stacked, index):
        tile = index // TILE
        height = stacked.shape[0] // 4
        got = stacked[3 * height:]
        for t in range(3):
            got = jnp.where(tile == t, stacked[t * height:(t + 1) * height], got)
        return got

    def to_tiles(values, index):
        tile = index // TILE
        return jnp.concatenate(
            [jnp.where(tile == t, values, 0.0).astype(BF16) for t in range(4)], axis=0
        )

    def side_by_side(stacked):
        height = stacked.shape[0] // 4
        return jnp.concatenate([stacked[t * height:(t + 1) * height] for t in range(4)], axis=1)

    for load in loads[:4]:
        load.wait()

    @pl.loop(0, rows // TILE)
    def _(j):
        cols = pl.ds(pl.multiple_of(j * TILE, TILE), TILE)
        got = dot(wt_ref[...], feat[:, cols]).astype(BF16)
        mapped[:, cols] = got
        mapped_tiles[pl.ds(pl.multiple_of(j * width, width), width), :] = got

    pl.semaphore_wait(barrier, BLOCKS - 1 + HIDS - 1)

    to_right = remote(mapped, near.at[0], n1_send.at[0], n1_recv.at[0], dom=right)
    to_left = remote(mapped, near.at[1], n1_send.at[1], n1_recv.at[1], dom=left)
    to_right.start()
    to_left.start()

    def pick(dz):
        index = list_row(send_ref, dz)
        picks[dz] = onehot(index)
        got = from_tiles(dot(mapped_tiles[...], picks[dz]), index).astype(BF16)
        for h in range(2):
            for i in range(LISTS):
                out1[h, LISTS * dz + i] = got[h * half:(h + 1) * half, i * 128:(i + 1) * 128]

    def buffers(first):
        return (out1, in1, a1_send, a1_recv) if first else (out2, in2, a2_send, a2_recv)

    def ship(first, h, dz, dy, c):
        outs, ins, ssem, rsem = buffers(first)
        back = lax.rem(ZS - dz, ZS)
        return remote(
            outs.at[h, LISTS * dz + 2 * dy + c], ins.at[h, LISTS * back + 2 * dy + core],
            ssem.at[h], rsem.at[h, back], dom=2 * chip_at(dz, dy) + c,
        )

    def sent(first, h):
        outs, ins, ssem, rsem = buffers(first)
        every = pl.ds(1, BLOCKS - 1)
        remote(outs.at[h, every], ins.at[h, every], ssem.at[h], rsem.at[h, 0], dom=left).wait_send()

    def ship_four(first, h, dz):
        for dy in (1, 0):
            for c in range(2):
                ship(first, h, dz, dy, c).start()

    def ship_near(first, h):
        outs, ins, _, _ = buffers(first)
        for c in range(2):
            ship(first, h, 0, 1, c).start()
        ship(first, h, 0, 0, 1 - core).start()
        ins[h, core] = outs[h, core]

    def arrive(first, h, dz, count):
        outs, ins, ssem, rsem = buffers(first)
        these = pl.ds(LISTS * dz, count)
        remote(outs.at[h, these], ins.at[h, these], ssem.at[h], rsem.at[h, dz], dom=left).wait_recv()

    def arrive_four(first, h, dz):
        arrive(first, h, dz, LISTS)

    def arrive_near(first, h):
        arrive(first, h, 0, LISTS - 1)

    @pl.loop(0, ZS - 1)
    def _(step):
        dz = offset(step)
        pick(dz)
        ship_four(True, 0, dz)

    pick(0)
    ship_near(True, 0)

    @pl.loop(0, ZS - 1)
    def _(step):
        ship_four(True, 1, offset(step))

    ship_near(True, 1)

    for load in loads[4:]:
        load.wait()

    wt = wt_ref[...]
    wsend[...] = jnp.zeros_like(wsend)
    for p in range(HIDS):
        wsend[p, :, :width] = wt[:, p * width:(p + 1) * width]
    wrecv[0] = wsend[hid]

    def hid_at(dl, dx):
        return lax.rem(hid // XS + dl, 2) * XS + lax.rem(lax.rem(hid, XS) + dx, XS)

    for dl in range(2):
        for dx in range(XS):
            if dl + dx:
                peer = hid_at(dl, dx)
                remote(wsend.at[peer], wrecv.at[XS * dl + (XS - dx) % XS], w_send.at[0], w_recv.at[0], hid=peer).start()

    slot_ids = lax.broadcasted_iota(jnp.int32, (BLOCKS, 128), 1).astype(F32)
    counts = row_to_column(slots_ref[...].astype(F32), BLOCKS)
    weights[...] = jnp.where(slot_ids < counts, ew_ref[...], 0.0)

    def dense_forward(source, s):
        @pl.loop(0, rows // TILE)
        def _(j):
            cols = pl.ds(pl.multiple_of(j * TILE, TILE), TILE)
            parts = [
                (source[:, t * TILE:(t + 1) * TILE].astype(F32)
                 * live_ref[j, s * 4 + t].astype(F32)).astype(BF16)
                for t in range(rows // TILE)
            ]
            got = dot(jnp.concatenate(parts, axis=1), band[s * rows:(s + 1) * rows, cols])
            if s == 1:
                acc[:, cols] = got
            else:
                acc[:, cols] += got

    dense_forward(mapped, 1)

    @pl.loop(0, ZS)
    def _(dz):
        puts[dz] = onehot(list_row(recv_ref, dz))

    to_right.wait_recv()
    dense_forward(near.at[0], 0)
    to_left.wait_recv()
    dense_forward(near.at[1], 2)

    bias_in_col = row_to_column(bias_ref[...], width)

    def lists_in(ins, h, dz):
        return jnp.concatenate([ins[h, LISTS * dz + i] for i in range(LISTS)], axis=1).astype(F32)

    def put(h, dz):
        values = lists_in(in1, h, dz) * list_row(weights, dz)
        sparse[h] += dot_nt(to_tiles(values, list_row(recv_ref, dz)), puts[dz])

    def activate(h):
        part = slice(h * half, (h + 1) * half)
        sparse[h] = jnp.zeros_like(sparse[h])

        @pl.loop(0, ZS - 1)
        def _(step):
            dz = offset(step)
            arrive_four(True, h, dz)
            put(h, dz)

        arrive_near(True, h)
        put(h, 0)
        act = acc[part] + bias_in_col[part] + side_by_side(sparse[h])
        gate = 1.0 / (1.0 + jnp.exp(-act))
        out_ref[part] = (act * gate).astype(BF16)
        grad = (cot[part].astype(F32) * (gate * (1.0 + act * (1.0 - gate)))).astype(BF16)
        pre[part] = grad
        for t in range(4):
            pre_tiles[h, t * half:(t + 1) * half] = grad[:, t * TILE:(t + 1) * TILE]

    def message(h, dz):
        got = from_tiles(dot(pre_tiles[h], puts[dz]), list_row(recv_ref, dz))
        got = (got * list_row(weights, dz)).astype(BF16)
        for i in range(LISTS):
            out2[h, LISTS * dz + i] = got[:, i * 128:(i + 1) * 128]

    def send_messages(h):
        @pl.loop(0, ZS - 1)
        def _(step):
            dz = offset(step)
            message(h, dz)
            ship_four(False, h, dz)

        message(h, 0)
        ship_near(False, h)

    def dense_backward(h, target, s):
        part = slice(h * half, (h + 1) * half)

        @pl.loop(0, rows // TILE)
        def _(t):
            cols = pl.ds(pl.multiple_of(t * TILE, TILE), TILE)
            parts = [
                (pre[part, j * TILE:(j + 1) * TILE].astype(F32)
                 * live_ref[j, s * 4 + t].astype(F32)).astype(BF16)
                for j in range(rows // TILE)
            ]
            band_rows = pl.ds(pl.multiple_of(s * rows + t * TILE, TILE), TILE)
            got = dot_nt(jnp.concatenate(parts, axis=1), band[band_rows, :])
            target[part, cols] = got.astype(target.dtype)

    def grad_move(h, side):
        part = pl.ds(h * half, half)
        return remote(
            term.at[side, part], term_in.at[side, part], n2_send.at[h, side], n2_recv.at[h, side],
            dom=(left, right)[side],
        )

    def dense_gradients(h):
        for side in range(2):
            dense_backward(h, term.at[side], 2 * side)
            grad_move(h, side).start()

    def bias_copy(step):
        bit = 1 << step
        peer = me + bit * (1 - 2 * lax.rem(me // bit, 2))
        return remote(bias_out.at[step], bias_in.at[step], b_send.at[step], b_recv.at[step], dom=peer)

    def bias_step(step):
        bias_copy(step).wait_recv()
        bias_out[step + 1] = bias_out[step] + bias_in[step]
        if step < 4:
            bias_copy(step + 1).start()

    activate(0)
    send_messages(0)
    dense_gradients(0)
    dense_backward(0, acc, 1)
    activate(1)
    send_messages(1)
    bias_col = jnp.sum(pre[...].astype(F32), axis=1, keepdims=True)
    diagonal = lax.broadcasted_iota(jnp.int32, (width, 128), 0) == lax.broadcasted_iota(jnp.int32, (width, 128), 1)
    bias_row = jnp.sum(jnp.where(diagonal, bias_col, 0.0), axis=0, keepdims=True)
    bias_out[0] = jnp.broadcast_to(bias_row, (8, 128))
    bias_copy(0).start()
    dense_gradients(1)
    bias_step(0)
    dense_backward(1, acc, 1)

    peers = pl.ds(1, HIDS - 1)
    slices = remote(wsend.at[peers], wrecv.at[peers], w_send.at[0], w_recv.at[0], dom=left)
    slices.wait_recv()
    slices.wait_send()

    wfull[...] = jnp.transpose(
        wrecv[...].reshape(HIDS * width, 128).astype(F32), (1, 0)
    )[:width].astype(BF16)

    def give_back(h, dz):
        sparse[h] += dot_nt(to_tiles(lists_in(in2, h, dz), list_row(send_ref, dz)), picks[dz])

    def gradient(h):
        part = slice(h * half, (h + 1) * half)
        sparse[h] = jnp.zeros_like(sparse[h])

        @pl.loop(0, ZS - 1)
        def _(step):
            dz = offset(step)
            arrive_four(False, h, dz)
            give_back(h, dz)

        arrive_near(False, h)
        give_back(h, 0)
        for side in range(2):
            grad_move(h, side).wait_recv()
        dense = acc[part] + (term_in[0, part].astype(F32) + term_in[1, part].astype(F32))
        gb[0, part] = (dense + side_by_side(sparse[h])).astype(BF16)

    def move(h, kind, src, dst, **where):
        part = pl.ds(h * half, half)
        return remote(gb.at[src, part], gb.at[dst, part], g_send.at[h, kind], g_recv.at[h, kind], **where)

    def share(h):
        move(h, 0, 0, XS, hid=hid_at(1, 0)).start()
        for dx in (2, 1, 3):
            move(h, 1, 0, XS - dx, hid=hid_at(0, dx)).start()

    def forward(h):
        move(h, 0, 0, XS, dom=left).wait_recv()
        for dx in (2, 1, 3):
            move(h, 2, XS, 2 * XS - dx, hid=hid_at(0, dx)).start()

    def shared(h, kind):
        these = pl.ds(1 if kind == 1 else XS + 1, XS - 1)
        return move(h, kind, these, these, dom=left)

    gradient(0)
    share(0)
    forward(0)
    gradient(1)

    wg = dot_nt(gb[0], feat[...])
    for d in range(BLOCKS):
        r, c = d // 4, d % 4
        pieces[d] = wg[8 * r:8 * r + 8, 128 * c:128 * c + 128].astype(BF16)

    def reduce_piece(j):
        peer = lax.rem(me + j, BLOCKS)
        return remote(pieces.at[peer], pieces_in.at[BLOCKS - j], rs_send.at[0], rs_recv.at[0], dom=peer)

    def spread_piece(j):
        return remote(summed, wg_all.at[me], ag_send.at[0], ag_recv.at[0], dom=lax.rem(me + j, BLOCKS))

    @pl.loop(1, BLOCKS)
    def _(j):
        reduce_piece(j).start()

    share(1)
    bias_step(1)
    forward(1)
    bias_step(2)
    for h in range(2):
        sent(True, h)
        sent(False, h)

    pieces_in[0] = pieces[me]
    others = pl.ds(1, BLOCKS - 1)
    reduced = remote(pieces.at[others], pieces_in.at[others], rs_send.at[0], rs_recv.at[0], dom=left)
    reduced.wait_recv()
    summed[...] = jnp.sum(pieces_in[...].astype(F32), axis=0).astype(BF16)

    @pl.loop(1, BLOCKS)
    def _(j):
        spread_piece(j).start()

    wg_all[me] = summed[...]
    bias_step(3)
    reduced.wait_send()

    for h in range(2):
        for kind in (1, 2):
            shared(h, kind).wait_recv()

    @pl.loop(0, rows // TILE)
    def _(j):
        cols = pl.ds(pl.multiple_of(j * TILE, TILE), TILE)
        stack = gb[:, :, cols].reshape(HIDS * width, TILE)
        fg_ref[:, cols] = dot(wfull[...], stack).astype(BF16)

    bias_step(4)
    bg_ref[...] = bias_out[5, 0:1, :width]

    spread = remote(pieces.at[others], wg_all.at[others], ag_send.at[0], ag_recv.at[0], dom=left)
    spread.wait_recv()

    for d in range(BLOCKS):
        r, c = d // 4, d % 4
        wg_ref[8 * r:8 * r + 8, 128 * c:128 * c + 128] = wg_all[d].astype(F32)

    to_right.wait_send()
    to_left.wait_send()
    for step in range(5):
        bias_copy(step).wait_send()

    for h in range(2):
        move(h, 0, 0, XS, dom=left).wait_send()
        for side in range(2):
            grad_move(h, side).wait_send()
            shared(h, side + 1).wait_send()
    spread.wait_send()


def finish(*refs):
    sources, targets, sem = refs[:4], refs[4:8], refs[8]
    copies = [
        pltpu.make_async_copy(src, dst, sem.at[i])
        for i, (src, dst) in enumerate(zip(sources, targets))
    ]
    for copy in copies:
        copy.start()
    for copy in copies:
        copy.wait()


def on_device(
    features,
    weight,
    band_tiles,
    tile_live,
    send_rows,
    recv_rows,
    edge_weight,
    live_slots,
    bias_terms,
    cotangent,
):
    depth, rows = features.shape
    width = weight.shape[1]
    vmem = pl.BlockSpec(memory_space=pltpu.VMEM)
    hbm = pl.BlockSpec(memory_space=pltpu.HBM)
    dma = pltpu.SemaphoreType.DMA
    block = pltpu.VMEM((width, rows), BF16)
    lists = pltpu.VMEM((2, BLOCKS, width // 2, 128), BF16)
    results = (((width, rows), BF16), ((width, rows), BF16), ((width, depth), F32), ((1, width), F32))
    parts = pl.pallas_call(
        kernel,
        out_shape=tuple(pltpu.VMEM(*r) for r in results),
        in_specs=[hbm] * 10,
        out_specs=(vmem,) * 4,
        scratch_shapes=[
            pltpu.VMEM((width, depth), BF16),
            pltpu.VMEM((depth, rows), BF16),
            pltpu.VMEM((3 * rows, rows), BF16),
            pltpu.SMEM((4, 12), jnp.int32),
            pltpu.VMEM((BLOCKS, 128), jnp.int32),
            pltpu.VMEM((BLOCKS, 128), jnp.int32),
            pltpu.VMEM((BLOCKS, 128), F32),
            pltpu.VMEM((1, BLOCKS), jnp.int32),
            pltpu.VMEM((1, width), F32),
            block,
            block,
            pltpu.VMEM((4 * width, TILE), BF16),
            pltpu.VMEM((2, width, rows), BF16),
            pltpu.VMEM((ZS, TILE, LISTS * 128), BF16),
            pltpu.VMEM((ZS, TILE, LISTS * 128), BF16),
            pltpu.VMEM((BLOCKS, 128), F32),
            pltpu.VMEM((width, rows), F32),
            pltpu.VMEM((2, 2 * width, TILE), F32),
            block,
            pltpu.VMEM((2, 2 * width, TILE), BF16),
            pltpu.VMEM((2, width, rows), BF16),
            pltpu.VMEM((2, width, rows), BF16),
            lists,
            lists,
            lists,
            lists,
            pltpu.VMEM((HIDS, width, 128), BF16),
            pltpu.VMEM((HIDS, width, 128), BF16),
            pltpu.VMEM((width, HIDS * width), BF16),
            pltpu.VMEM((HIDS, width, rows), BF16),
            pltpu.VMEM((6, 8, 128), F32),
            pltpu.VMEM((5, 8, 128), F32),
            pltpu.VMEM((BLOCKS, 8, 128), BF16),
            pltpu.VMEM((BLOCKS, 8, 128), BF16),
            pltpu.VMEM((8, 128), BF16),
            pltpu.VMEM((BLOCKS, 8, 128), BF16),
            dma((10,)),
            dma((2,)),
            dma((2, ZS)),
            dma((2,)),
            dma((2,)),
            dma((2,)),
            dma((2, ZS)),
            dma((2, 2)),
            dma((2, 2)),
            dma((1,)),
            dma((1,)),
            dma((5,)),
            dma((5,)),
            dma((2, 3)),
            dma((2, 3)),
            dma((1,)),
            dma((1,)),
            dma((1,)),
            dma((1,)),
        ],
        compiler_params=pltpu.CompilerParams(
            collective_id=0, has_side_effects=True, vmem_limit_bytes=56 << 20
        ),
    )(
        weight.T,
        features,
        band_tiles,
        tile_live.T,
        send_rows[0],
        recv_rows[0],
        edge_weight[0],
        live_slots,
        bias_terms.reshape(1, width),
        cotangent,
    )
    output, feature_grad, wg, bg = pl.pallas_call(
        finish,
        out_shape=tuple(jax.ShapeDtypeStruct(*r) for r in results),
        in_specs=[vmem] * 4,
        out_specs=(hbm,) * 4,
        scratch_shapes=[dma((4,))],
        compiler_params=pltpu.CompilerParams(vmem_limit_bytes=4 << 20),
    )(*parts)
    return (output, feature_grad, wg.T, bg.reshape(width))


def solution(mesh):
    return jax.shard_map(
        on_device,
        mesh=mesh,
        in_specs=(
            P(None, "dom"),
            P(None, "hid"),
            P(None, "dom"),
            P(None, "dom"),
            P("dom", None, None),
            P("dom", None, None),
            P("dom", None, None),
            P("dom", None),
            P("hid"),
            P("hid", "dom"),
        ),
        out_specs=(P("hid", "dom"), P("hid", "dom"), P(None, "hid"), P("hid")),
        check_vma=False,
    )
```

```python
import jax
import jax.numpy as jnp
from jax import lax
from jax.experimental import pallas as pl
from jax.experimental.pallas import tpu as pltpu
from jax.sharding import PartitionSpec as P

MESH = pl.DeviceIdType.MESH
F32 = jnp.float32
BF16 = jnp.bfloat16
TILE = 256
NT = (((1,), (1,)), ((), ()))
ZS = 8
LISTS = 4
PARTS = ((0, 32), (32, 32))
BLOCKS = 32
HIDS = 8
XS = 4
ARRIVALS = ((4, 3, 5), (2, 6, 1), (7, 0))
DEPARTURES = ((4, 3), (5, 2), (6, 1), (7,))


def dot(a, b):
    return jnp.dot(a, b, preferred_element_type=F32)


def dot_nt(a, b):
    return lax.dot_general(a, b, NT, preferred_element_type=F32)


def row_to_column(row, rows):
    lanes = row.shape[1]
    at = lax.broadcasted_iota(jnp.int32, (rows, lanes), 0)
    to = lax.broadcasted_iota(jnp.int32, (rows, lanes), 1)
    return jnp.sum(jnp.where(at == to, row, 0.0), axis=1, keepdims=True)


def kernel(
    wt_hbm,
    feat_hbm,
    band_hbm,
    live_hbm,
    send_hbm,
    recv_hbm,
    ew_hbm,
    slots_hbm,
    bias_hbm,
    cot_hbm,
    out_ref,
    fg_ref,
    wg_ref,
    bg_ref,
    wt_ref,
    feat,
    band,
    live_ref,
    send_ref,
    recv_ref,
    ew_ref,
    slots_ref,
    bias_ref,
    cot,
    mapped,
    mapped_tiles,
    near,
    picks,
    puts,
    weights,
    acc,
    pre,
    pre_tiles,
    term,
    term_in,
    out1,
    in1,
    out2,
    in2,
    wsend,
    wrecv,
    wfull,
    gb,
    bias_out,
    bias_in,
    pieces,
    pieces_in,
    summed,
    wg_all,
    load_sem,
    a1_send,
    a1_recv,
    n1_send,
    n1_recv,
    a2_send,
    a2_recv,
    n2_send,
    n2_recv,
    w_send,
    w_recv,
    b_send,
    b_recv,
    g_send,
    g_recv,
    rs_send,
    rs_recv,
    ag_send,
    ag_recv,
):
    me = lax.axis_index("dom")
    hid = lax.axis_index("hid")
    core = lax.rem(me, 2)
    z = lax.rem(me // 2, ZS)
    yh = me // (2 * ZS)
    left = lax.rem(me + BLOCKS - 1, BLOCKS)
    right = lax.rem(me + 1, BLOCKS)
    rows = mapped.shape[1]
    width = mapped.shape[0]
    half = width // 2
    barrier = pltpu.get_barrier_semaphore()

    @pl.loop(1, BLOCKS)
    def _(j):
        pl.semaphore_signal(barrier, inc=1, device_id={"dom": lax.rem(me + j, BLOCKS)}, device_id_type=MESH)

    @pl.loop(1, HIDS)
    def _(j):
        pl.semaphore_signal(barrier, inc=1, device_id={"hid": lax.rem(hid + j, HIDS)}, device_id_type=MESH)

    loads = [
        pltpu.make_async_copy(src, dst, load_sem.at[i])
        for i, (src, dst) in enumerate((
            (wt_hbm, wt_ref), (feat_hbm, feat), (send_hbm, send_ref), (slots_hbm, slots_ref),
            (ew_hbm, ew_ref), (recv_hbm, recv_ref), (bias_hbm, bias_ref), (live_hbm, live_ref),
            (band_hbm, band), (cot_hbm, cot),
        ))
    ]
    for load in loads:
        load.start()

    def remote(src, dst, ssem, rsem, **where):
        return pltpu.make_async_remote_copy(
            src_ref=src, dst_ref=dst, send_sem=ssem, recv_sem=rsem,
            device_id=where, device_id_type=MESH,
        )

    def offset(step):
        far = (step + 1) // 2
        return lax.rem(4 + far * (1 - 2 * lax.rem(step, 2)) + ZS, ZS)

    def chip_at(dz, dy):
        return lax.rem(yh + dy, 2) * ZS + lax.rem(z + dz, ZS)

    def list_row(ref, dz):
        return jnp.concatenate(
            [ref[pl.ds(2 * chip_at(dz, dy) + c, 1), :] for dy in range(2) for c in range(2)], axis=1
        )

    def onehot(index):
        at = lax.broadcasted_iota(jnp.int32, (TILE, LISTS * 128), 0)
        return jnp.where(at == index % TILE, 1.0, 0.0).astype(BF16)

    def from_tiles(stacked, index):
        tile = index // TILE
        height = stacked.shape[0] // 4
        got = stacked[3 * height:]
        for t in range(3):
            got = jnp.where(tile == t, stacked[t * height:(t + 1) * height], got)
        return got

    def to_tiles(values, index):
        tile = index // TILE
        return jnp.concatenate(
            [jnp.where(tile == t, values, 0.0).astype(BF16) for t in range(4)], axis=0
        )

    def side_by_side(stacked):
        height = stacked.shape[0] // 4
        return jnp.concatenate([stacked[t * height:(t + 1) * height] for t in range(4)], axis=1)

    for load in loads[:4]:
        load.wait()

    @pl.loop(0, rows // TILE)
    def _(j):
        cols = pl.ds(pl.multiple_of(j * TILE, TILE), TILE)
        got = dot(wt_ref[...], feat[:, cols]).astype(BF16)
        mapped[:, cols] = got
        mapped_tiles[pl.ds(pl.multiple_of(j * width, width), width), :] = got

    pl.semaphore_wait(barrier, BLOCKS - 1 + HIDS - 1)

    to_right = remote(mapped, near.at[0], n1_send.at[0], n1_recv.at[0], dom=right)
    to_left = remote(mapped, near.at[1], n1_send.at[1], n1_recv.at[1], dom=left)
    to_right.start()
    to_left.start()

    def pick(dz):
        index = list_row(send_ref, dz)
        picks[dz] = onehot(index)
        got = from_tiles(dot(mapped_tiles[...], picks[dz]), index).astype(BF16)
        for i in range(LISTS):
            out1[LISTS * dz + i] = got[:, i * 128:(i + 1) * 128]

    def buffers(first):
        return (out1, in1, a1_send, a1_recv) if first else (out2, in2, a2_send, a2_recv)

    def ship(first, p, dz, dy, c):
        outs, ins, ssem, rsem = buffers(first)
        back = lax.rem(ZS - dz, ZS)
        part = pl.ds(*PARTS[p])
        return remote(
            outs.at[LISTS * dz + 2 * dy + c, part], ins.at[LISTS * back + 2 * dy + core, part],
            ssem.at[p], rsem.at[p, back], dom=2 * chip_at(dz, dy) + c,
        )

    def sent(first, p):
        outs, ins, ssem, rsem = buffers(first)
        every, part = pl.ds(1, BLOCKS - 1), pl.ds(*PARTS[p])
        remote(outs.at[every, part], ins.at[every, part], ssem.at[p], rsem.at[p, 0], dom=left).wait_send()

    def ship_four(first, p, dz):
        for dy in (1, 0):
            for c in range(2):
                ship(first, p, dz, dy, c).start()

    def ship_near(first, p):
        outs, ins, _, _ = buffers(first)
        part = pl.ds(*PARTS[p])
        for c in range(2):
            ship(first, p, 0, 1, c).start()
        ship(first, p, 0, 0, 1 - core).start()
        ins[core, part] = outs[core, part]

    def arrive(first, p, dz, count):
        outs, ins, ssem, rsem = buffers(first)
        these, part = pl.ds(LISTS * dz, count), pl.ds(*PARTS[p])
        remote(outs.at[these, part], ins.at[these, part], ssem.at[p], rsem.at[p, dz], dom=left).wait_recv()

    for batch in DEPARTURES:
        for dz in batch:
            pick(dz)
        for dz in batch:
            ship_four(True, 0, dz)

    pick(0)
    ship_near(True, 0)
    for p in range(1, len(PARTS)):
        @pl.loop(0, ZS - 1)
        def _(step):
            ship_four(True, p, offset(step))

        ship_near(True, p)

    for load in loads[4:]:
        load.wait()

    wt = wt_ref[...]
    wsend[...] = jnp.zeros_like(wsend)
    for p in range(HIDS):
        wsend[p, :, :width] = wt[:, p * width:(p + 1) * width]
    wrecv[0] = wsend[hid]

    def hid_at(dl, dx):
        return lax.rem(hid // XS + dl, 2) * XS + lax.rem(lax.rem(hid, XS) + dx, XS)

    for dl in range(2):
        for dx in range(XS):
            if dl + dx:
                peer = hid_at(dl, dx)
                remote(wsend.at[peer], wrecv.at[XS * dl + (XS - dx) % XS], w_send.at[0], w_recv.at[0], hid=peer).start()

    slot_ids = lax.broadcasted_iota(jnp.int32, (BLOCKS, 128), 1).astype(F32)
    counts = row_to_column(slots_ref[...].astype(F32), BLOCKS)
    weights[...] = jnp.where(slot_ids < counts, ew_ref[...], 0.0)

    def dense_forward(source, s):
        @pl.loop(0, rows // TILE)
        def _(j):
            cols = pl.ds(pl.multiple_of(j * TILE, TILE), TILE)
            parts = [
                (source[:, t * TILE:(t + 1) * TILE].astype(F32)
                 * live_ref[j, s * 4 + t].astype(F32)).astype(BF16)
                for t in range(rows // TILE)
            ]
            got = dot(jnp.concatenate(parts, axis=1), band[s * rows:(s + 1) * rows, cols])
            if s == 1:
                acc[:, cols] = got
            else:
                acc[:, cols] += got

    dense_forward(mapped, 1)

    @pl.loop(0, ZS)
    def _(dz):
        puts[dz] = onehot(list_row(recv_ref, dz))

    to_right.wait_recv()
    dense_forward(near.at[0], 0)
    to_left.wait_recv()
    dense_forward(near.at[1], 2)

    bias_in_col = row_to_column(bias_ref[...], width)

    def lists_in(ins, p, dz):
        part = pl.ds(*PARTS[p])
        return jnp.concatenate([ins[LISTS * dz + i, part] for i in range(LISTS)], axis=1).astype(F32)

    def stacked(p):
        return slice(4 * PARTS[p][0], 4 * (PARTS[p][0] + PARTS[p][1]))

    def collect(first, p, part_of):
        total = None
        for batch in ARRIVALS:
            for dz in batch:
                arrive(first, p, dz, LISTS if dz else LISTS - 1)
            for dz in batch:
                got = part_of(p, dz)
                total = got if total is None else total + got
        return side_by_side(total)

    def put(p, dz):
        values = lists_in(in1, p, dz) * list_row(weights, dz)
        return dot_nt(to_tiles(values, list_row(recv_ref, dz)), puts[dz])

    def activate(p):
        start, size = PARTS[p]
        part = slice(start, start + size)
        act = collect(True, p, put) + acc[part] + bias_in_col[part]
        gate = 1.0 / (1.0 + jnp.exp(-act))
        out_ref[part] = (act * gate).astype(BF16)
        grad = (cot[part].astype(F32) * (gate * (1.0 + act * (1.0 - gate)))).astype(BF16)
        pre[part] = grad
        for t in range(4):
            pre_tiles[4 * start + t * size:4 * start + (t + 1) * size] = grad[:, t * TILE:(t + 1) * TILE]

    def message(p, dz):
        got = from_tiles(dot(pre_tiles[stacked(p)], puts[dz]), list_row(recv_ref, dz))
        got = (got * list_row(weights, dz)).astype(BF16)
        for i in range(LISTS):
            out2[LISTS * dz + i, pl.ds(*PARTS[p])] = got[:, i * 128:(i + 1) * 128]

    def send_messages(p):
        for batch in DEPARTURES:
            for dz in batch:
                message(p, dz)
            for dz in batch:
                ship_four(False, p, dz)

        message(p, 0)
        ship_near(False, p)

    def dense_backward(h, target, s):
        part = slice(h * half, (h + 1) * half)

        @pl.loop(0, rows // TILE)
        def _(t):
            cols = pl.ds(pl.multiple_of(t * TILE, TILE), TILE)
            parts = [
                (pre[part, j * TILE:(j + 1) * TILE].astype(F32)
                 * live_ref[j, s * 4 + t].astype(F32)).astype(BF16)
                for j in range(rows // TILE)
            ]
            band_rows = pl.ds(pl.multiple_of(s * rows + t * TILE, TILE), TILE)
            got = dot_nt(jnp.concatenate(parts, axis=1), band[band_rows, :])
            target[part, cols] = got.astype(target.dtype)

    def grad_move(h, side):
        part = pl.ds(h * half, half)
        return remote(
            term.at[side, part], term_in.at[side, part], n2_send.at[h, side], n2_recv.at[h, side],
            dom=(left, right)[side],
        )

    def dense_gradients(h):
        for side in range(2):
            dense_backward(h, term.at[side], 2 * side)
            grad_move(h, side).start()

    def bias_copy(step):
        bit = 1 << step
        peer = me + bit * (1 - 2 * lax.rem(me // bit, 2))
        return remote(bias_out.at[step], bias_in.at[step], b_send.at[step], b_recv.at[step], dom=peer)

    def bias_step(step):
        bias_copy(step).wait_recv()
        bias_out[step + 1] = bias_out[step] + bias_in[step]
        if step < 4:
            bias_copy(step + 1).start()

    for p, (start, size) in enumerate(PARTS):
        activate(p)
        send_messages(p)
        if start + size == half:
            dense_gradients(0)
            dense_backward(0, acc, 1)

    bias_col = jnp.sum(pre[...].astype(F32), axis=1, keepdims=True)
    diagonal = lax.broadcasted_iota(jnp.int32, (width, 128), 0) == lax.broadcasted_iota(jnp.int32, (width, 128), 1)
    bias_row = jnp.sum(jnp.where(diagonal, bias_col, 0.0), axis=0, keepdims=True)
    bias_out[0] = jnp.broadcast_to(bias_row, (8, 128))
    bias_copy(0).start()
    dense_gradients(1)
    bias_step(0)
    dense_backward(1, acc, 1)

    peers = pl.ds(1, HIDS - 1)
    slices = remote(wsend.at[peers], wrecv.at[peers], w_send.at[0], w_recv.at[0], dom=left)
    slices.wait_recv()
    slices.wait_send()

    wfull[...] = jnp.transpose(
        wrecv[...].reshape(HIDS * width, 128).astype(F32), (1, 0)
    )[:width].astype(BF16)

    def give_back(p, dz):
        return dot_nt(to_tiles(lists_in(in2, p, dz), list_row(send_ref, dz)), picks[dz])

    def gradient(p):
        start, size = PARTS[p]
        part = slice(start, start + size)
        returned = collect(False, p, give_back)
        if start % half == 0:
            for side in range(2):
                grad_move(start // half, side).wait_recv()
        dense = acc[part] + (term_in[0, part].astype(F32) + term_in[1, part].astype(F32))
        gb[0, part] = (dense + returned).astype(BF16)

    def move(h, kind, src, dst, **where):
        part = pl.ds(h * half, half)
        return remote(gb.at[src, part], gb.at[dst, part], g_send.at[h, kind], g_recv.at[h, kind], **where)

    def share(h):
        move(h, 0, 0, XS, hid=hid_at(1, 0)).start()
        for dx in (2, 1, 3):
            move(h, 1, 0, XS - dx, hid=hid_at(0, dx)).start()

    def forward(h):
        move(h, 0, 0, XS, dom=left).wait_recv()
        for dx in (2, 1, 3):
            move(h, 2, XS, 2 * XS - dx, hid=hid_at(0, dx)).start()

    def shared(h, kind):
        these = pl.ds(1 if kind == 1 else XS + 1, XS - 1)
        return move(h, kind, these, these, dom=left)

    for p, (start, size) in enumerate(PARTS):
        gradient(p)
        if start + size == half:
            share(0)
            forward(0)

    wg = dot_nt(gb[0], feat[...])
    for d in range(BLOCKS):
        r, c = d // 4, d % 4
        pieces[d] = wg[8 * r:8 * r + 8, 128 * c:128 * c + 128].astype(BF16)

    def reduce_piece(j):
        peer = lax.rem(me + j, BLOCKS)
        return remote(pieces.at[peer], pieces_in.at[BLOCKS - j], rs_send.at[0], rs_recv.at[0], dom=peer)

    def spread_piece(j):
        return remote(summed, wg_all.at[me], ag_send.at[0], ag_recv.at[0], dom=lax.rem(me + j, BLOCKS))

    @pl.loop(1, BLOCKS)
    def _(j):
        reduce_piece(j).start()

    share(1)
    bias_step(1)
    forward(1)
    bias_step(2)
    for p in range(len(PARTS)):
        sent(True, p)
        sent(False, p)

    pieces_in[0] = pieces[me]
    others = pl.ds(1, BLOCKS - 1)
    reduced = remote(pieces.at[others], pieces_in.at[others], rs_send.at[0], rs_recv.at[0], dom=left)
    reduced.wait_recv()
    summed[...] = jnp.sum(pieces_in[...].astype(F32), axis=0).astype(BF16)

    @pl.loop(1, BLOCKS)
    def _(j):
        spread_piece(j).start()

    wg_all[me] = summed[...]
    bias_step(3)
    reduced.wait_send()

    for h in range(2):
        for kind in (1, 2):
            shared(h, kind).wait_recv()

    @pl.loop(0, rows // TILE)
    def _(j):
        cols = pl.ds(pl.multiple_of(j * TILE, TILE), TILE)
        stack = gb[:, :, cols].reshape(HIDS * width, TILE)
        fg_ref[:, cols] = dot(wfull[...], stack).astype(BF16)

    bias_step(4)
    bg_ref[...] = bias_out[5, 0:1, :width]

    spread = remote(pieces.at[others], wg_all.at[others], ag_send.at[0], ag_recv.at[0], dom=left)
    spread.wait_recv()

    for d in range(BLOCKS):
        r, c = d // 4, d % 4
        wg_ref[8 * r:8 * r + 8, 128 * c:128 * c + 128] = wg_all[d].astype(F32)

    to_right.wait_send()
    to_left.wait_send()
    for step in range(5):
        bias_copy(step).wait_send()

    for h in range(2):
        move(h, 0, 0, XS, dom=left).wait_send()
        for side in range(2):
            grad_move(h, side).wait_send()
            shared(h, side + 1).wait_send()
    spread.wait_send()


def finish(*refs):
    sources, targets, sem = refs[:4], refs[4:8], refs[8]
    copies = [
        pltpu.make_async_copy(src, dst, sem.at[i])
        for i, (src, dst) in enumerate(zip(sources, targets))
    ]
    for copy in copies:
        copy.start()
    for copy in copies:
        copy.wait()


def on_device(
    features,
    weight,
    band_tiles,
    tile_live,
    send_rows,
    recv_rows,
    edge_weight,
    live_slots,
    bias_terms,
    cotangent,
):
    depth, rows = features.shape
    width = weight.shape[1]
    vmem = pl.BlockSpec(memory_space=pltpu.VMEM)
    hbm = pl.BlockSpec(memory_space=pltpu.HBM)
    dma = pltpu.SemaphoreType.DMA
    block = pltpu.VMEM((width, rows), BF16)
    lists = pltpu.VMEM((BLOCKS, width, 128), BF16)
    results = (((width, rows), BF16), ((width, rows), BF16), ((width, depth), F32), ((1, width), F32))
    parts = pl.pallas_call(
        kernel,
        out_shape=tuple(pltpu.VMEM(*r) for r in results),
        in_specs=[hbm] * 10,
        out_specs=(vmem,) * 4,
        scratch_shapes=[
            pltpu.VMEM((width, depth), BF16),
            pltpu.VMEM((depth, rows), BF16),
            pltpu.VMEM((3 * rows, rows), BF16),
            pltpu.SMEM((4, 12), jnp.int32),
            pltpu.VMEM((BLOCKS, 128), jnp.int32),
            pltpu.VMEM((BLOCKS, 128), jnp.int32),
            pltpu.VMEM((BLOCKS, 128), F32),
            pltpu.VMEM((1, BLOCKS), jnp.int32),
            pltpu.VMEM((1, width), F32),
            block,
            block,
            pltpu.VMEM((4 * width, TILE), BF16),
            pltpu.VMEM((2, width, rows), BF16),
            pltpu.VMEM((ZS, TILE, LISTS * 128), BF16),
            pltpu.VMEM((ZS, TILE, LISTS * 128), BF16),
            pltpu.VMEM((BLOCKS, 128), F32),
            pltpu.VMEM((width, rows), F32),
            block,
            pltpu.VMEM((4 * width, TILE), BF16),
            pltpu.VMEM((2, width, rows), BF16),
            pltpu.VMEM((2, width, rows), BF16),
            lists,
            lists,
            lists,
            lists,
            pltpu.VMEM((HIDS, width, 128), BF16),
            pltpu.VMEM((HIDS, width, 128), BF16),
            pltpu.VMEM((width, HIDS * width), BF16),
            pltpu.VMEM((HIDS, width, rows), BF16),
            pltpu.VMEM((6, 8, 128), F32),
            pltpu.VMEM((5, 8, 128), F32),
            pltpu.VMEM((BLOCKS, 8, 128), BF16),
            pltpu.VMEM((BLOCKS, 8, 128), BF16),
            pltpu.VMEM((8, 128), BF16),
            pltpu.VMEM((BLOCKS, 8, 128), BF16),
            dma((10,)),
            dma((len(PARTS),)),
            dma((len(PARTS), ZS)),
            dma((2,)),
            dma((2,)),
            dma((len(PARTS),)),
            dma((len(PARTS), ZS)),
            dma((2, 2)),
            dma((2, 2)),
            dma((1,)),
            dma((1,)),
            dma((5,)),
            dma((5,)),
            dma((2, 3)),
            dma((2, 3)),
            dma((1,)),
            dma((1,)),
            dma((1,)),
            dma((1,)),
        ],
        compiler_params=pltpu.CompilerParams(
            collective_id=0, has_side_effects=True, vmem_limit_bytes=56 << 20
        ),
    )(
        weight.T,
        features,
        band_tiles,
        tile_live.T,
        send_rows[0],
        recv_rows[0],
        edge_weight[0],
        live_slots,
        bias_terms.reshape(1, width),
        cotangent,
    )
    output, feature_grad, wg, bg = pl.pallas_call(
        finish,
        out_shape=tuple(jax.ShapeDtypeStruct(*r) for r in results),
        in_specs=[vmem] * 4,
        out_specs=(hbm,) * 4,
        scratch_shapes=[dma((4,))],
        compiler_params=pltpu.CompilerParams(vmem_limit_bytes=4 << 20),
    )(*parts)
    return (output, feature_grad, wg.T, bg.reshape(width))


def solution(mesh):
    return jax.shard_map(
        on_device,
        mesh=mesh,
        in_specs=(
            P(None, "dom"),
            P(None, "hid"),
            P(None, "dom"),
            P(None, "dom"),
            P("dom", None, None),
            P("dom", None, None),
            P("dom", None, None),
            P("dom", None),
            P("hid"),
            P("hid", "dom"),
        ),
        out_specs=(P("hid", "dom"), P("hid", "dom"), P(None, "hid"), P("hid")),
        check_vma=False,
    )
```

```python
import jax
import jax.numpy as jnp
from jax import lax
from jax.experimental import pallas as pl
from jax.experimental.pallas import tpu as pltpu
from jax.sharding import PartitionSpec as P

MESH = pl.DeviceIdType.MESH
F32 = jnp.float32
BF16 = jnp.bfloat16
TILE = 256
NT = (((1,), (1,)), ((), ()))
ZS = 8
LISTS = 4
PARTS = ((0, 32), (32, 32))
BLOCKS = 32
HIDS = 8
XS = 4
ARRIVALS = ((4, 3, 5), (2, 6, 1), (7, 0))
DEPARTURES = ((4, 3), (5, 2), (6, 1), (7,))


def dot(a, b):
    return jnp.dot(a, b, preferred_element_type=F32)


def dot_nt(a, b):
    return lax.dot_general(a, b, NT, preferred_element_type=F32)


def row_to_column(row, rows):
    lanes = row.shape[1]
    at = lax.broadcasted_iota(jnp.int32, (rows, lanes), 0)
    to = lax.broadcasted_iota(jnp.int32, (rows, lanes), 1)
    return jnp.sum(jnp.where(at == to, row, 0.0), axis=1, keepdims=True)


def kernel(
    wt_hbm,
    feat_hbm,
    band_hbm,
    live_hbm,
    send_hbm,
    recv_hbm,
    ew_hbm,
    slots_hbm,
    bias_hbm,
    cot_hbm,
    out_ref,
    fg_ref,
    wg_ref,
    bg_ref,
    wt_ref,
    feat,
    band,
    live_ref,
    send_ref,
    recv_ref,
    ew_ref,
    slots_ref,
    bias_ref,
    cot,
    mapped,
    mapped_tiles,
    near,
    picks,
    puts,
    weights,
    acc,
    pre,
    pre_tiles,
    term,
    term_in,
    out1,
    in1,
    out2,
    in2,
    wsend,
    wrecv,
    wfull,
    gb,
    bias_out,
    bias_in,
    pieces,
    pieces_in,
    summed,
    wg_all,
    load_sem,
    a1_send,
    a1_recv,
    n1_send,
    n1_recv,
    a2_send,
    a2_recv,
    n2_send,
    n2_recv,
    w_send,
    w_recv,
    b_send,
    b_recv,
    g_send,
    g_recv,
    rs_send,
    rs_recv,
    ag_send,
    ag_recv,
):
    me = lax.axis_index("dom")
    hid = lax.axis_index("hid")
    core = lax.rem(me, 2)
    z = lax.rem(me // 2, ZS)
    yh = me // (2 * ZS)
    left = lax.rem(me + BLOCKS - 1, BLOCKS)
    right = lax.rem(me + 1, BLOCKS)
    rows = mapped.shape[1]
    width = mapped.shape[0]
    half = width // 2
    barrier = pltpu.get_barrier_semaphore()

    @pl.loop(1, BLOCKS)
    def _(j):
        pl.semaphore_signal(barrier, inc=1, device_id={"dom": lax.rem(me + j, BLOCKS)}, device_id_type=MESH)

    @pl.loop(1, HIDS)
    def _(j):
        pl.semaphore_signal(barrier, inc=1, device_id={"hid": lax.rem(hid + j, HIDS)}, device_id_type=MESH)

    loads = [
        pltpu.make_async_copy(src, dst, load_sem.at[i])
        for i, (src, dst) in enumerate((
            (wt_hbm, wt_ref), (feat_hbm, feat), (send_hbm, send_ref), (slots_hbm, slots_ref),
            (ew_hbm, ew_ref), (recv_hbm, recv_ref), (bias_hbm, bias_ref), (live_hbm, live_ref),
            (band_hbm, band), (cot_hbm, cot),
        ))
    ]
    for load in loads:
        load.start()

    def remote(src, dst, ssem, rsem, **where):
        return pltpu.make_async_remote_copy(
            src_ref=src, dst_ref=dst, send_sem=ssem, recv_sem=rsem,
            device_id=where, device_id_type=MESH,
        )

    def offset(step):
        far = (step + 1) // 2
        return lax.rem(4 + far * (1 - 2 * lax.rem(step, 2)) + ZS, ZS)

    def chip_at(dz, dy):
        return lax.rem(yh + dy, 2) * ZS + lax.rem(z + dz, ZS)

    def list_row(ref, dz):
        return jnp.concatenate(
            [ref[pl.ds(2 * chip_at(dz, dy) + c, 1), :] for dy in range(2) for c in range(2)], axis=1
        )

    def onehot(index):
        at = lax.broadcasted_iota(jnp.int32, (TILE, LISTS * 128), 0)
        return jnp.where(at == index % TILE, 1.0, 0.0).astype(BF16)

    def from_tiles(stacked, index):
        tile = index // TILE
        height = stacked.shape[0] // 4
        got = stacked[3 * height:]
        for t in range(3):
            got = jnp.where(tile == t, stacked[t * height:(t + 1) * height], got)
        return got

    def to_tiles(values, index):
        tile = index // TILE
        return jnp.concatenate(
            [jnp.where(tile == t, values, 0.0).astype(BF16) for t in range(4)], axis=0
        )

    def side_by_side(stacked):
        height = stacked.shape[0] // 4
        return jnp.concatenate([stacked[t * height:(t + 1) * height] for t in range(4)], axis=1)

    for load in loads[:4]:
        load.wait()

    @pl.loop(0, rows // TILE)
    def _(j):
        cols = pl.ds(pl.multiple_of(j * TILE, TILE), TILE)
        got = dot(wt_ref[...], feat[:, cols]).astype(BF16)
        mapped[:, cols] = got
        mapped_tiles[pl.ds(pl.multiple_of(j * width, width), width), :] = got

    pl.semaphore_wait(barrier, BLOCKS - 1 + HIDS - 1)

    to_right = remote(mapped, near.at[0], n1_send.at[0], n1_recv.at[0], dom=right)
    to_left = remote(mapped, near.at[1], n1_send.at[1], n1_recv.at[1], dom=left)
    to_right.start()
    to_left.start()

    def pick(dz):
        index = list_row(send_ref, dz)
        picks[dz] = onehot(index)
        got = from_tiles(dot(mapped_tiles[...], picks[dz]), index).astype(BF16)
        for i in range(LISTS):
            out1[LISTS * dz + i] = got[:, i * 128:(i + 1) * 128]

    def buffers(first):
        return (out1, in1, a1_send, a1_recv) if first else (out2, in2, a2_send, a2_recv)

    def ship(first, p, dz, dy, c):
        outs, ins, ssem, rsem = buffers(first)
        back = lax.rem(ZS - dz, ZS)
        part = pl.ds(*PARTS[p])
        return remote(
            outs.at[LISTS * dz + 2 * dy + c, part], ins.at[LISTS * back + 2 * dy + core, part],
            ssem.at[p], rsem.at[p, back], dom=2 * chip_at(dz, dy) + c,
        )

    def sent(first, p):
        outs, ins, ssem, rsem = buffers(first)
        every, part = pl.ds(1, BLOCKS - 1), pl.ds(*PARTS[p])
        remote(outs.at[every, part], ins.at[every, part], ssem.at[p], rsem.at[p, 0], dom=left).wait_send()

    def ship_four(first, p, dz):
        for dy in (1, 0):
            for c in range(2):
                ship(first, p, dz, dy, c).start()

    def ship_near(first, p):
        outs, ins, _, _ = buffers(first)
        part = pl.ds(*PARTS[p])
        for c in range(2):
            ship(first, p, 0, 1, c).start()
        ship(first, p, 0, 0, 1 - core).start()
        ins[core, part] = outs[core, part]

    def arrive(first, p, dz, count):
        outs, ins, ssem, rsem = buffers(first)
        these, part = pl.ds(LISTS * dz, count), pl.ds(*PARTS[p])
        remote(outs.at[these, part], ins.at[these, part], ssem.at[p], rsem.at[p, dz], dom=left).wait_recv()

    for batch in DEPARTURES:
        for dz in batch:
            pick(dz)
        for dz in batch:
            ship_four(True, 0, dz)

    pick(0)
    ship_near(True, 0)
    for p in range(1, len(PARTS)):
        @pl.loop(0, ZS - 1)
        def _(step):
            ship_four(True, p, offset(step))

        ship_near(True, p)

    for load in loads[4:]:
        load.wait()

    wt = wt_ref[...]
    wsend[...] = jnp.zeros_like(wsend)
    for p in range(HIDS):
        wsend[p, :, :width] = wt[:, p * width:(p + 1) * width]
    wrecv[0] = wsend[hid]

    def hid_at(dl, dx):
        return lax.rem(hid // XS + dl, 2) * XS + lax.rem(lax.rem(hid, XS) + dx, XS)

    for dl in range(2):
        for dx in range(XS):
            if dl + dx:
                peer = hid_at(dl, dx)
                remote(wsend.at[peer], wrecv.at[XS * dl + (XS - dx) % XS], w_send.at[0], w_recv.at[0], hid=peer).start()

    slot_ids = lax.broadcasted_iota(jnp.int32, (BLOCKS, 128), 1).astype(F32)
    counts = row_to_column(slots_ref[...].astype(F32), BLOCKS)
    weights[...] = jnp.where(slot_ids < counts, ew_ref[...], 0.0)

    def dense_forward(source, s):
        @pl.loop(0, rows // TILE)
        def _(j):
            cols = pl.ds(pl.multiple_of(j * TILE, TILE), TILE)
            parts = [
                (source[:, t * TILE:(t + 1) * TILE].astype(F32)
                 * live_ref[j, s * 4 + t].astype(F32)).astype(BF16)
                for t in range(rows // TILE)
            ]
            got = dot(jnp.concatenate(parts, axis=1), band[s * rows:(s + 1) * rows, cols])
            if s == 1:
                acc[:, cols] = got
            else:
                acc[:, cols] += got

    dense_forward(mapped, 1)

    @pl.loop(0, ZS)
    def _(dz):
        puts[dz] = onehot(list_row(recv_ref, dz))

    to_right.wait_recv()
    dense_forward(near.at[0], 0)
    to_left.wait_recv()
    dense_forward(near.at[1], 2)

    bias_in_col = row_to_column(bias_ref[...], width)

    def lists_in(ins, p, dz):
        part = pl.ds(*PARTS[p])
        return jnp.concatenate([ins[LISTS * dz + i, part] for i in range(LISTS)], axis=1).astype(F32)

    def stacked(p):
        return slice(4 * PARTS[p][0], 4 * (PARTS[p][0] + PARTS[p][1]))

    def collect(first, p, part_of, then=None):
        total = None
        for batch in ARRIVALS:
            if then is not None and batch is ARRIVALS[1]:
                then()
            for dz in batch:
                arrive(first, p, dz, LISTS if dz else LISTS - 1)
            for dz in batch:
                got = part_of(p, dz)
                total = got if total is None else total + got
        return side_by_side(total)

    def put(p, dz):
        values = lists_in(in1, p, dz) * list_row(weights, dz)
        return dot_nt(to_tiles(values, list_row(recv_ref, dz)), puts[dz])

    def activate(p):
        start, size = PARTS[p]
        part = slice(start, start + size)
        act = collect(True, p, put) + acc[part] + bias_in_col[part]
        gate = 1.0 / (1.0 + jnp.exp(-act))
        out_ref[part] = (act * gate).astype(BF16)
        grad = (cot[part].astype(F32) * (gate * (1.0 + act * (1.0 - gate)))).astype(BF16)
        pre[part] = grad
        for t in range(4):
            pre_tiles[4 * start + t * size:4 * start + (t + 1) * size] = grad[:, t * TILE:(t + 1) * TILE]

    def message(p, dz):
        got = from_tiles(dot(pre_tiles[stacked(p)], puts[dz]), list_row(recv_ref, dz))
        got = (got * list_row(weights, dz)).astype(BF16)
        for i in range(LISTS):
            out2[LISTS * dz + i, pl.ds(*PARTS[p])] = got[:, i * 128:(i + 1) * 128]

    def send_messages(p):
        for batch in DEPARTURES:
            for dz in batch:
                message(p, dz)
            for dz in batch:
                ship_four(False, p, dz)

        message(p, 0)
        ship_near(False, p)

    def dense_backward(h, target, s):
        part = slice(h * half, (h + 1) * half)

        @pl.loop(0, rows // TILE)
        def _(t):
            cols = pl.ds(pl.multiple_of(t * TILE, TILE), TILE)
            parts = [
                (pre[part, j * TILE:(j + 1) * TILE].astype(F32)
                 * live_ref[j, s * 4 + t].astype(F32)).astype(BF16)
                for j in range(rows // TILE)
            ]
            band_rows = pl.ds(pl.multiple_of(s * rows + t * TILE, TILE), TILE)
            got = dot_nt(jnp.concatenate(parts, axis=1), band[band_rows, :])
            target[part, cols] = got.astype(target.dtype)

    def grad_move(h, side):
        part = pl.ds(h * half, half)
        return remote(
            term.at[side, part], term_in.at[side, part], n2_send.at[h, side], n2_recv.at[h, side],
            dom=(left, right)[side],
        )

    def dense_gradients(h):
        for side in range(2):
            dense_backward(h, term.at[side], 2 * side)
            grad_move(h, side).start()

    def bias_copy(step):
        bit = 1 << step
        peer = me + bit * (1 - 2 * lax.rem(me // bit, 2))
        return remote(bias_out.at[step], bias_in.at[step], b_send.at[step], b_recv.at[step], dom=peer)

    def bias_step(step):
        bias_copy(step).wait_recv()
        bias_out[step + 1] = bias_out[step] + bias_in[step]
        if step < 4:
            bias_copy(step + 1).start()

    for p, (start, size) in enumerate(PARTS):
        activate(p)
        send_messages(p)
        if start + size == half:
            dense_gradients(0)
            dense_backward(0, acc, 1)

    bias_col = jnp.sum(pre[...].astype(F32), axis=1, keepdims=True)
    diagonal = lax.broadcasted_iota(jnp.int32, (width, 128), 0) == lax.broadcasted_iota(jnp.int32, (width, 128), 1)
    bias_row = jnp.sum(jnp.where(diagonal, bias_col, 0.0), axis=0, keepdims=True)
    bias_out[0] = jnp.broadcast_to(bias_row, (8, 128))
    bias_copy(0).start()
    dense_gradients(1)
    bias_step(0)
    dense_backward(1, acc, 1)

    peers = pl.ds(1, HIDS - 1)
    slices = remote(wsend.at[peers], wrecv.at[peers], w_send.at[0], w_recv.at[0], dom=left)
    slices.wait_recv()
    slices.wait_send()

    wfull[...] = jnp.transpose(
        wrecv[...].reshape(HIDS * width, 128).astype(F32), (1, 0)
    )[:width].astype(BF16)

    def give_back(p, dz):
        return dot_nt(to_tiles(lists_in(in2, p, dz), list_row(send_ref, dz)), picks[dz])

    def gradient(p, then=None):
        start, size = PARTS[p]
        part = slice(start, start + size)
        returned = collect(False, p, give_back, then)
        if start % half == 0:
            for side in range(2):
                grad_move(start // half, side).wait_recv()
        dense = acc[part] + (term_in[0, part].astype(F32) + term_in[1, part].astype(F32))
        gb[0, part] = (dense + returned).astype(BF16)

    def move(h, kind, src, dst, **where):
        part = pl.ds(h * half, half)
        return remote(gb.at[src, part], gb.at[dst, part], g_send.at[h, kind], g_recv.at[h, kind], **where)

    def share(h):
        move(h, 0, 0, XS, hid=hid_at(1, 0)).start()
        for dx in (2, 1, 3):
            move(h, 1, 0, XS - dx, hid=hid_at(0, dx)).start()

    def forward(h):
        move(h, 0, 0, XS, dom=left).wait_recv()
        for dx in (2, 1, 3):
            move(h, 2, XS, 2 * XS - dx, hid=hid_at(0, dx)).start()

    def shared(h, kind):
        these = pl.ds(1 if kind == 1 else XS + 1, XS - 1)
        return move(h, kind, these, these, dom=left)

    for p, (start, size) in enumerate(PARTS):
        gradient(p, (lambda: forward(0)) if start == half else None)
        if start + size == half:
            share(0)

    wg = dot_nt(gb[0], feat[...])
    for d in range(BLOCKS):
        r, c = d // 4, d % 4
        pieces[d] = wg[8 * r:8 * r + 8, 128 * c:128 * c + 128].astype(BF16)

    def reduce_piece(j):
        peer = lax.rem(me + j, BLOCKS)
        return remote(pieces.at[peer], pieces_in.at[BLOCKS - j], rs_send.at[0], rs_recv.at[0], dom=peer)

    def spread_piece(j):
        return remote(summed, wg_all.at[me], ag_send.at[0], ag_recv.at[0], dom=lax.rem(me + j, BLOCKS))

    @pl.loop(1, BLOCKS)
    def _(j):
        reduce_piece(j).start()

    share(1)
    bias_step(1)
    forward(1)
    bias_step(2)
    for p in range(len(PARTS)):
        sent(True, p)
        sent(False, p)

    pieces_in[0] = pieces[me]
    others = pl.ds(1, BLOCKS - 1)
    reduced = remote(pieces.at[others], pieces_in.at[others], rs_send.at[0], rs_recv.at[0], dom=left)
    reduced.wait_recv()
    summed[...] = jnp.sum(pieces_in[...].astype(F32), axis=0).astype(BF16)

    @pl.loop(1, BLOCKS)
    def _(j):
        spread_piece(j).start()

    wg_all[me] = summed[...]
    bias_step(3)
    reduced.wait_send()

    for h in range(2):
        for kind in (1, 2):
            shared(h, kind).wait_recv()

    @pl.loop(0, rows // TILE)
    def _(j):
        cols = pl.ds(pl.multiple_of(j * TILE, TILE), TILE)
        stack = gb[:, :, cols].reshape(HIDS * width, TILE)
        fg_ref[:, cols] = dot(wfull[...], stack).astype(BF16)

    bias_step(4)
    bg_ref[...] = bias_out[5, 0:1, :width]

    spread = remote(pieces.at[others], wg_all.at[others], ag_send.at[0], ag_recv.at[0], dom=left)
    spread.wait_recv()

    for d in range(BLOCKS):
        r, c = d // 4, d % 4
        wg_ref[8 * r:8 * r + 8, 128 * c:128 * c + 128] = wg_all[d].astype(F32)

    to_right.wait_send()
    to_left.wait_send()
    for step in range(5):
        bias_copy(step).wait_send()

    for h in range(2):
        move(h, 0, 0, XS, dom=left).wait_send()
        for side in range(2):
            grad_move(h, side).wait_send()
            shared(h, side + 1).wait_send()
    spread.wait_send()


def finish(*refs):
    sources, targets, sem = refs[:4], refs[4:8], refs[8]
    copies = [
        pltpu.make_async_copy(src, dst, sem.at[i])
        for i, (src, dst) in enumerate(zip(sources, targets))
    ]
    for copy in copies:
        copy.start()
    for copy in copies:
        copy.wait()


def on_device(
    features,
    weight,
    band_tiles,
    tile_live,
    send_rows,
    recv_rows,
    edge_weight,
    live_slots,
    bias_terms,
    cotangent,
):
    depth, rows = features.shape
    width = weight.shape[1]
    vmem = pl.BlockSpec(memory_space=pltpu.VMEM)
    hbm = pl.BlockSpec(memory_space=pltpu.HBM)
    dma = pltpu.SemaphoreType.DMA
    block = pltpu.VMEM((width, rows), BF16)
    lists = pltpu.VMEM((BLOCKS, width, 128), BF16)
    results = (((width, rows), BF16), ((width, rows), BF16), ((width, depth), F32), ((1, width), F32))
    parts = pl.pallas_call(
        kernel,
        out_shape=tuple(pltpu.VMEM(*r) for r in results),
        in_specs=[hbm] * 10,
        out_specs=(vmem,) * 4,
        scratch_shapes=[
            pltpu.VMEM((width, depth), BF16),
            pltpu.VMEM((depth, rows), BF16),
            pltpu.VMEM((3 * rows, rows), BF16),
            pltpu.SMEM((4, 12), jnp.int32),
            pltpu.VMEM((BLOCKS, 128), jnp.int32),
            pltpu.VMEM((BLOCKS, 128), jnp.int32),
            pltpu.VMEM((BLOCKS, 128), F32),
            pltpu.VMEM((1, BLOCKS), jnp.int32),
            pltpu.VMEM((1, width), F32),
            block,
            block,
            pltpu.VMEM((4 * width, TILE), BF16),
            pltpu.VMEM((2, width, rows), BF16),
            pltpu.VMEM((ZS, TILE, LISTS * 128), BF16),
            pltpu.VMEM((ZS, TILE, LISTS * 128), BF16),
            pltpu.VMEM((BLOCKS, 128), F32),
            pltpu.VMEM((width, rows), F32),
            block,
            pltpu.VMEM((4 * width, TILE), BF16),
            pltpu.VMEM((2, width, rows), BF16),
            pltpu.VMEM((2, width, rows), BF16),
            lists,
            lists,
            lists,
            lists,
            pltpu.VMEM((HIDS, width, 128), BF16),
            pltpu.VMEM((HIDS, width, 128), BF16),
            pltpu.VMEM((width, HIDS * width), BF16),
            pltpu.VMEM((HIDS, width, rows), BF16),
            pltpu.VMEM((6, 8, 128), F32),
            pltpu.VMEM((5, 8, 128), F32),
            pltpu.VMEM((BLOCKS, 8, 128), BF16),
            pltpu.VMEM((BLOCKS, 8, 128), BF16),
            pltpu.VMEM((8, 128), BF16),
            pltpu.VMEM((BLOCKS, 8, 128), BF16),
            dma((10,)),
            dma((len(PARTS),)),
            dma((len(PARTS), ZS)),
            dma((2,)),
            dma((2,)),
            dma((len(PARTS),)),
            dma((len(PARTS), ZS)),
            dma((2, 2)),
            dma((2, 2)),
            dma((1,)),
            dma((1,)),
            dma((5,)),
            dma((5,)),
            dma((2, 3)),
            dma((2, 3)),
            dma((1,)),
            dma((1,)),
            dma((1,)),
            dma((1,)),
        ],
        compiler_params=pltpu.CompilerParams(
            collective_id=0, has_side_effects=True, vmem_limit_bytes=56 << 20
        ),
    )(
        weight.T,
        features,
        band_tiles,
        tile_live.T,
        send_rows[0],
        recv_rows[0],
        edge_weight[0],
        live_slots,
        bias_terms.reshape(1, width),
        cotangent,
    )
    output, feature_grad, wg, bg = pl.pallas_call(
        finish,
        out_shape=tuple(jax.ShapeDtypeStruct(*r) for r in results),
        in_specs=[vmem] * 4,
        out_specs=(hbm,) * 4,
        scratch_shapes=[dma((4,))],
        compiler_params=pltpu.CompilerParams(vmem_limit_bytes=4 << 20),
    )(*parts)
    return (output, feature_grad, wg.T, bg.reshape(width))


def solution(mesh):
    return jax.shard_map(
        on_device,
        mesh=mesh,
        in_specs=(
            P(None, "dom"),
            P(None, "hid"),
            P(None, "dom"),
            P(None, "dom"),
            P("dom", None, None),
            P("dom", None, None),
            P("dom", None, None),
            P("dom", None),
            P("hid"),
            P("hid", "dom"),
        ),
        out_specs=(P("hid", "dom"), P("hid", "dom"), P(None, "hid"), P("hid")),
        check_vma=False,
    )
```

```python
import jax
import jax.numpy as jnp
from jax import lax
from jax.experimental import pallas as pl
from jax.experimental.pallas import tpu as pltpu
from jax.sharding import PartitionSpec as P

MESH = pl.DeviceIdType.MESH
F32 = jnp.float32
BF16 = jnp.bfloat16
TILE = 256
NT = (((1,), (1,)), ((), ()))
ZS = 8
LISTS = 4
PARTS = ((0, 32), (32, 32))
BLOCKS = 32
HIDS = 8
XS = 4
ARRIVALS = ((4, 3, 5), (2, 6, 1), (7, 0))
DEPARTURES = ((4, 3), (5, 2), (6, 1), (7,))


def dot(a, b):
    return jnp.dot(a, b, preferred_element_type=F32)


def dot_nt(a, b):
    return lax.dot_general(a, b, NT, preferred_element_type=F32)


def row_to_column(row, rows):
    lanes = row.shape[1]
    at = lax.broadcasted_iota(jnp.int32, (rows, lanes), 0)
    to = lax.broadcasted_iota(jnp.int32, (rows, lanes), 1)
    return jnp.sum(jnp.where(at == to, row, 0.0), axis=1, keepdims=True)


def kernel(
    wt_hbm,
    feat_hbm,
    band_hbm,
    live_hbm,
    send_hbm,
    recv_hbm,
    ew_hbm,
    slots_hbm,
    bias_hbm,
    cot_hbm,
    out_ref,
    fg_ref,
    wg_ref,
    bg_ref,
    wt_ref,
    feat,
    band,
    live_ref,
    send_ref,
    recv_ref,
    ew_ref,
    slots_ref,
    bias_ref,
    cot,
    mapped,
    mapped_tiles,
    near,
    picks,
    puts,
    weights,
    acc,
    pre,
    pre_tiles,
    term,
    term_in,
    out1,
    in1,
    out2,
    in2,
    wsend,
    wrecv,
    wfull,
    gb,
    bias_out,
    bias_in,
    pieces,
    pieces_in,
    summed,
    wg_all,
    load_sem,
    a1_send,
    a1_recv,
    n1_send,
    n1_recv,
    a2_send,
    a2_recv,
    n2_send,
    n2_recv,
    w_send,
    w_recv,
    b_send,
    b_recv,
    g_send,
    g_recv,
    rs_send,
    rs_recv,
    ag_send,
    ag_recv,
):
    me = lax.axis_index("dom")
    hid = lax.axis_index("hid")
    core = lax.rem(me, 2)
    z = lax.rem(me // 2, ZS)
    yh = me // (2 * ZS)
    left = lax.rem(me + BLOCKS - 1, BLOCKS)
    right = lax.rem(me + 1, BLOCKS)
    rows = mapped.shape[1]
    width = mapped.shape[0]
    half = width // 2
    barrier = pltpu.get_barrier_semaphore()

    @pl.loop(1, BLOCKS)
    def _(j):
        pl.semaphore_signal(barrier, inc=1, device_id={"dom": lax.rem(me + j, BLOCKS)}, device_id_type=MESH)

    @pl.loop(1, HIDS)
    def _(j):
        pl.semaphore_signal(barrier, inc=1, device_id={"hid": lax.rem(hid + j, HIDS)}, device_id_type=MESH)

    loads = [
        pltpu.make_async_copy(src, dst, load_sem.at[i])
        for i, (src, dst) in enumerate((
            (wt_hbm, wt_ref), (feat_hbm, feat), (send_hbm, send_ref), (slots_hbm, slots_ref),
            (ew_hbm, ew_ref), (recv_hbm, recv_ref), (bias_hbm, bias_ref), (live_hbm, live_ref),
            (band_hbm, band), (cot_hbm, cot),
        ))
    ]
    for load in loads:
        load.start()

    def remote(src, dst, ssem, rsem, **where):
        return pltpu.make_async_remote_copy(
            src_ref=src, dst_ref=dst, send_sem=ssem, recv_sem=rsem,
            device_id=where, device_id_type=MESH,
        )

    def offset(step):
        far = (step + 1) // 2
        return lax.rem(4 + far * (1 - 2 * lax.rem(step, 2)) + ZS, ZS)

    def chip_at(dz, dy):
        return lax.rem(yh + dy, 2) * ZS + lax.rem(z + dz, ZS)

    def list_row(ref, dz):
        return jnp.concatenate(
            [ref[pl.ds(2 * chip_at(dz, dy) + c, 1), :] for dy in range(2) for c in range(2)], axis=1
        )

    def onehot(index):
        at = lax.broadcasted_iota(jnp.int32, (TILE, LISTS * 128), 0)
        return jnp.where(at == index % TILE, 1.0, 0.0).astype(BF16)

    def from_tiles(stacked, index):
        tile = index // TILE
        height = stacked.shape[0] // 4
        got = stacked[3 * height:]
        for t in range(3):
            got = jnp.where(tile == t, stacked[t * height:(t + 1) * height], got)
        return got

    def to_tiles(values, index):
        tile = index // TILE
        return jnp.concatenate(
            [jnp.where(tile == t, values, 0.0).astype(BF16) for t in range(4)], axis=0
        )

    def side_by_side(stacked):
        height = stacked.shape[0] // 4
        return jnp.concatenate([stacked[t * height:(t + 1) * height] for t in range(4)], axis=1)

    for load in loads[:6]:
        load.wait()

    @pl.loop(0, rows // TILE)
    def _(j):
        cols = pl.ds(pl.multiple_of(j * TILE, TILE), TILE)
        got = dot(wt_ref[...], feat[:, cols]).astype(BF16)
        mapped[:, cols] = got
        mapped_tiles[pl.ds(pl.multiple_of(j * width, width), width), :] = got

    def pick(dz):
        index = list_row(send_ref, dz)
        picks[dz] = onehot(index)
        got = from_tiles(dot(mapped_tiles[...], picks[dz]), index).astype(BF16)
        for i in range(LISTS):
            out1[LISTS * dz + i] = got[:, i * 128:(i + 1) * 128]

    def buffers(first):
        return (out1, in1, a1_send, a1_recv) if first else (out2, in2, a2_send, a2_recv)

    def ship(first, p, dz, dy, c):
        outs, ins, ssem, rsem = buffers(first)
        back = lax.rem(ZS - dz, ZS)
        part = pl.ds(*PARTS[p])
        return remote(
            outs.at[LISTS * dz + 2 * dy + c, part], ins.at[LISTS * back + 2 * dy + core, part],
            ssem.at[p], rsem.at[p, back], dom=2 * chip_at(dz, dy) + c,
        )

    def sent(first, p):
        outs, ins, ssem, rsem = buffers(first)
        every, part = pl.ds(1, BLOCKS - 1), pl.ds(*PARTS[p])
        remote(outs.at[every, part], ins.at[every, part], ssem.at[p], rsem.at[p, 0], dom=left).wait_send()

    def ship_four(first, p, dz):
        for dy in (1, 0):
            for c in range(2):
                ship(first, p, dz, dy, c).start()

    def ship_near(first, p):
        outs, ins, _, _ = buffers(first)
        part = pl.ds(*PARTS[p])
        for c in range(2):
            ship(first, p, 0, 1, c).start()
        ship(first, p, 0, 0, 1 - core).start()
        ins[core, part] = outs[core, part]

    def arrive(first, p, dz, count):
        outs, ins, ssem, rsem = buffers(first)
        these, part = pl.ds(LISTS * dz, count), pl.ds(*PARTS[p])
        remote(outs.at[these, part], ins.at[these, part], ssem.at[p], rsem.at[p, dz], dom=left).wait_recv()

    for dz in range(ZS):
        pick(dz)

    @pl.loop(0, ZS)
    def _(dz):
        puts[dz] = onehot(list_row(recv_ref, dz))

    slot_ids = lax.broadcasted_iota(jnp.int32, (BLOCKS, 128), 1).astype(F32)
    counts = row_to_column(slots_ref[...].astype(F32), BLOCKS)
    weights[...] = jnp.where(slot_ids < counts, ew_ref[...], 0.0)

    wt = wt_ref[...]
    wsend[...] = jnp.zeros_like(wsend)
    for p in range(HIDS):
        wsend[p, :, :width] = wt[:, p * width:(p + 1) * width]
    wrecv[0] = wsend[hid]

    pl.semaphore_wait(barrier, BLOCKS - 1 + HIDS - 1)

    to_right = remote(mapped, near.at[0], n1_send.at[0], n1_recv.at[0], dom=right)
    to_left = remote(mapped, near.at[1], n1_send.at[1], n1_recv.at[1], dom=left)
    to_right.start()
    to_left.start()

    for p in range(len(PARTS)):
        @pl.loop(0, ZS - 1)
        def _(step):
            ship_four(True, p, offset(step))

        ship_near(True, p)

    for load in loads[6:]:
        load.wait()

    def hid_at(dl, dx):
        return lax.rem(hid // XS + dl, 2) * XS + lax.rem(lax.rem(hid, XS) + dx, XS)

    for dl in range(2):
        for dx in range(XS):
            if dl + dx:
                peer = hid_at(dl, dx)
                remote(wsend.at[peer], wrecv.at[XS * dl + (XS - dx) % XS], w_send.at[0], w_recv.at[0], hid=peer).start()

    def dense_forward(source, s):
        @pl.loop(0, rows // TILE)
        def _(j):
            cols = pl.ds(pl.multiple_of(j * TILE, TILE), TILE)
            parts = [
                (source[:, t * TILE:(t + 1) * TILE].astype(F32)
                 * live_ref[j, s * 4 + t].astype(F32)).astype(BF16)
                for t in range(rows // TILE)
            ]
            got = dot(jnp.concatenate(parts, axis=1), band[s * rows:(s + 1) * rows, cols])
            if s == 1:
                acc[:, cols] = got
            else:
                acc[:, cols] += got

    dense_forward(mapped, 1)

    to_right.wait_recv()
    dense_forward(near.at[0], 0)
    to_left.wait_recv()
    dense_forward(near.at[1], 2)

    bias_in_col = row_to_column(bias_ref[...], width)

    def lists_in(ins, p, dz):
        part = pl.ds(*PARTS[p])
        return jnp.concatenate([ins[LISTS * dz + i, part] for i in range(LISTS)], axis=1).astype(F32)

    def stacked(p):
        return slice(4 * PARTS[p][0], 4 * (PARTS[p][0] + PARTS[p][1]))

    def collect(first, p, part_of, then=None):
        total = None
        for batch in ARRIVALS:
            if then is not None and batch is ARRIVALS[1]:
                then()
            for dz in batch:
                arrive(first, p, dz, LISTS if dz else LISTS - 1)
            for dz in batch:
                got = part_of(p, dz)
                total = got if total is None else total + got
        return side_by_side(total)

    def put(p, dz):
        values = lists_in(in1, p, dz) * list_row(weights, dz)
        return dot_nt(to_tiles(values, list_row(recv_ref, dz)), puts[dz])

    def activate(p):
        start, size = PARTS[p]
        part = slice(start, start + size)
        act = collect(True, p, put) + acc[part] + bias_in_col[part]
        gate = 1.0 / (1.0 + jnp.exp(-act))
        out_ref[part] = (act * gate).astype(BF16)
        grad = (cot[part].astype(F32) * (gate * (1.0 + act * (1.0 - gate)))).astype(BF16)
        pre[part] = grad
        for t in range(4):
            pre_tiles[4 * start + t * size:4 * start + (t + 1) * size] = grad[:, t * TILE:(t + 1) * TILE]

    def message(p, dz):
        got = from_tiles(dot(pre_tiles[stacked(p)], puts[dz]), list_row(recv_ref, dz))
        got = (got * list_row(weights, dz)).astype(BF16)
        for i in range(LISTS):
            out2[LISTS * dz + i, pl.ds(*PARTS[p])] = got[:, i * 128:(i + 1) * 128]

    def send_messages(p):
        for batch in DEPARTURES:
            for dz in batch:
                message(p, dz)
            for dz in batch:
                ship_four(False, p, dz)

        message(p, 0)
        ship_near(False, p)

    def dense_backward(h, target, s):
        part = slice(h * half, (h + 1) * half)

        @pl.loop(0, rows // TILE)
        def _(t):
            cols = pl.ds(pl.multiple_of(t * TILE, TILE), TILE)
            parts = [
                (pre[part, j * TILE:(j + 1) * TILE].astype(F32)
                 * live_ref[j, s * 4 + t].astype(F32)).astype(BF16)
                for j in range(rows // TILE)
            ]
            band_rows = pl.ds(pl.multiple_of(s * rows + t * TILE, TILE), TILE)
            got = dot_nt(jnp.concatenate(parts, axis=1), band[band_rows, :])
            target[part, cols] = got.astype(target.dtype)

    def grad_move(h, side):
        part = pl.ds(h * half, half)
        return remote(
            term.at[side, part], term_in.at[side, part], n2_send.at[h, side], n2_recv.at[h, side],
            dom=(left, right)[side],
        )

    def dense_gradients(h):
        for side in range(2):
            dense_backward(h, term.at[side], 2 * side)
            grad_move(h, side).start()

    def bias_copy(step):
        bit = 1 << step
        peer = me + bit * (1 - 2 * lax.rem(me // bit, 2))
        return remote(bias_out.at[step], bias_in.at[step], b_send.at[step], b_recv.at[step], dom=peer)

    def bias_step(step):
        bias_copy(step).wait_recv()
        bias_out[step + 1] = bias_out[step] + bias_in[step]
        if step < 4:
            bias_copy(step + 1).start()

    for p, (start, size) in enumerate(PARTS):
        activate(p)
        send_messages(p)
        if start + size == half:
            dense_gradients(0)
            dense_backward(0, acc, 1)

    bias_col = jnp.sum(pre[...].astype(F32), axis=1, keepdims=True)
    diagonal = lax.broadcasted_iota(jnp.int32, (width, 128), 0) == lax.broadcasted_iota(jnp.int32, (width, 128), 1)
    bias_row = jnp.sum(jnp.where(diagonal, bias_col, 0.0), axis=0, keepdims=True)
    bias_out[0] = jnp.broadcast_to(bias_row, (8, 128))
    bias_copy(0).start()
    dense_gradients(1)
    bias_step(0)
    dense_backward(1, acc, 1)

    peers = pl.ds(1, HIDS - 1)
    slices = remote(wsend.at[peers], wrecv.at[peers], w_send.at[0], w_recv.at[0], dom=left)
    slices.wait_recv()
    slices.wait_send()

    wfull[...] = jnp.transpose(
        wrecv[...].reshape(HIDS * width, 128).astype(F32), (1, 0)
    )[:width].astype(BF16)

    def give_back(p, dz):
        return dot_nt(to_tiles(lists_in(in2, p, dz), list_row(send_ref, dz)), picks[dz])

    def gradient(p, then=None):
        start, size = PARTS[p]
        part = slice(start, start + size)
        returned = collect(False, p, give_back, then)
        if start % half == 0:
            for side in range(2):
                grad_move(start // half, side).wait_recv()
        dense = acc[part] + (term_in[0, part].astype(F32) + term_in[1, part].astype(F32))
        gb[0, part] = (dense + returned).astype(BF16)

    def move(h, kind, src, dst, **where):
        part = pl.ds(h * half, half)
        return remote(gb.at[src, part], gb.at[dst, part], g_send.at[h, kind], g_recv.at[h, kind], **where)

    def share(h):
        move(h, 0, 0, XS, hid=hid_at(1, 0)).start()
        for dx in (2, 1, 3):
            move(h, 1, 0, XS - dx, hid=hid_at(0, dx)).start()

    def forward(h):
        move(h, 0, 0, XS, dom=left).wait_recv()
        for dx in (2, 1, 3):
            move(h, 2, XS, 2 * XS - dx, hid=hid_at(0, dx)).start()

    def shared(h, kind):
        these = pl.ds(1 if kind == 1 else XS + 1, XS - 1)
        return move(h, kind, these, these, dom=left)

    for p, (start, size) in enumerate(PARTS):
        gradient(p, (lambda: forward(0)) if start == half else None)
        if start + size == half:
            share(0)

    wg = dot_nt(gb[0], feat[...])
    for d in range(BLOCKS):
        r, c = d // 4, d % 4
        pieces[d] = wg[8 * r:8 * r + 8, 128 * c:128 * c + 128].astype(BF16)

    def reduce_piece(j):
        peer = lax.rem(me + j, BLOCKS)
        return remote(pieces.at[peer], pieces_in.at[BLOCKS - j], rs_send.at[0], rs_recv.at[0], dom=peer)

    def spread_piece(j):
        return remote(summed, wg_all.at[me], ag_send.at[0], ag_recv.at[0], dom=lax.rem(me + j, BLOCKS))

    @pl.loop(1, BLOCKS)
    def _(j):
        reduce_piece(j).start()

    share(1)
    bias_step(1)
    forward(1)
    bias_step(2)
    for p in range(len(PARTS)):
        sent(True, p)
        sent(False, p)

    pieces_in[0] = pieces[me]
    others = pl.ds(1, BLOCKS - 1)
    reduced = remote(pieces.at[others], pieces_in.at[others], rs_send.at[0], rs_recv.at[0], dom=left)
    reduced.wait_recv()
    summed[...] = jnp.sum(pieces_in[...].astype(F32), axis=0).astype(BF16)

    @pl.loop(1, BLOCKS)
    def _(j):
        spread_piece(j).start()

    wg_all[me] = summed[...]
    bias_step(3)
    reduced.wait_send()

    for h in range(2):
        for kind in (1, 2):
            shared(h, kind).wait_recv()

    @pl.loop(0, rows // TILE)
    def _(j):
        cols = pl.ds(pl.multiple_of(j * TILE, TILE), TILE)
        stack = gb[:, :, cols].reshape(HIDS * width, TILE)
        fg_ref[:, cols] = dot(wfull[...], stack).astype(BF16)

    bias_step(4)
    bg_ref[...] = bias_out[5, 0:1, :width]

    spread = remote(pieces.at[others], wg_all.at[others], ag_send.at[0], ag_recv.at[0], dom=left)
    spread.wait_recv()

    for d in range(BLOCKS):
        r, c = d // 4, d % 4
        wg_ref[8 * r:8 * r + 8, 128 * c:128 * c + 128] = wg_all[d].astype(F32)

    to_right.wait_send()
    to_left.wait_send()
    for step in range(5):
        bias_copy(step).wait_send()

    for h in range(2):
        move(h, 0, 0, XS, dom=left).wait_send()
        for side in range(2):
            grad_move(h, side).wait_send()
            shared(h, side + 1).wait_send()
    spread.wait_send()


def finish(*refs):
    sources, targets, sem = refs[:4], refs[4:8], refs[8]
    copies = [
        pltpu.make_async_copy(src, dst, sem.at[i])
        for i, (src, dst) in enumerate(zip(sources, targets))
    ]
    for copy in copies:
        copy.start()
    for copy in copies:
        copy.wait()


def on_device(
    features,
    weight,
    band_tiles,
    tile_live,
    send_rows,
    recv_rows,
    edge_weight,
    live_slots,
    bias_terms,
    cotangent,
):
    depth, rows = features.shape
    width = weight.shape[1]
    vmem = pl.BlockSpec(memory_space=pltpu.VMEM)
    hbm = pl.BlockSpec(memory_space=pltpu.HBM)
    dma = pltpu.SemaphoreType.DMA
    block = pltpu.VMEM((width, rows), BF16)
    lists = pltpu.VMEM((BLOCKS, width, 128), BF16)
    results = (((width, rows), BF16), ((width, rows), BF16), ((width, depth), F32), ((1, width), F32))
    parts = pl.pallas_call(
        kernel,
        out_shape=tuple(pltpu.VMEM(*r) for r in results),
        in_specs=[hbm] * 10,
        out_specs=(vmem,) * 4,
        scratch_shapes=[
            pltpu.VMEM((width, depth), BF16),
            pltpu.VMEM((depth, rows), BF16),
            pltpu.VMEM((3 * rows, rows), BF16),
            pltpu.SMEM((4, 12), jnp.int32),
            pltpu.VMEM((BLOCKS, 128), jnp.int32),
            pltpu.VMEM((BLOCKS, 128), jnp.int32),
            pltpu.VMEM((BLOCKS, 128), F32),
            pltpu.VMEM((1, BLOCKS), jnp.int32),
            pltpu.VMEM((1, width), F32),
            block,
            block,
            pltpu.VMEM((4 * width, TILE), BF16),
            pltpu.VMEM((2, width, rows), BF16),
            pltpu.VMEM((ZS, TILE, LISTS * 128), BF16),
            pltpu.VMEM((ZS, TILE, LISTS * 128), BF16),
            pltpu.VMEM((BLOCKS, 128), F32),
            pltpu.VMEM((width, rows), F32),
            block,
            pltpu.VMEM((4 * width, TILE), BF16),
            pltpu.VMEM((2, width, rows), BF16),
            pltpu.VMEM((2, width, rows), BF16),
            lists,
            lists,
            lists,
            lists,
            pltpu.VMEM((HIDS, width, 128), BF16),
            pltpu.VMEM((HIDS, width, 128), BF16),
            pltpu.VMEM((width, HIDS * width), BF16),
            pltpu.VMEM((HIDS, width, rows), BF16),
            pltpu.VMEM((6, 8, 128), F32),
            pltpu.VMEM((5, 8, 128), F32),
            pltpu.VMEM((BLOCKS, 8, 128), BF16),
            pltpu.VMEM((BLOCKS, 8, 128), BF16),
            pltpu.VMEM((8, 128), BF16),
            pltpu.VMEM((BLOCKS, 8, 128), BF16),
            dma((10,)),
            dma((len(PARTS),)),
            dma((len(PARTS), ZS)),
            dma((2,)),
            dma((2,)),
            dma((len(PARTS),)),
            dma((len(PARTS), ZS)),
            dma((2, 2)),
            dma((2, 2)),
            dma((1,)),
            dma((1,)),
            dma((5,)),
            dma((5,)),
            dma((2, 3)),
            dma((2, 3)),
            dma((1,)),
            dma((1,)),
            dma((1,)),
            dma((1,)),
        ],
        compiler_params=pltpu.CompilerParams(
            collective_id=0, has_side_effects=True, vmem_limit_bytes=56 << 20
        ),
    )(
        weight.T,
        features,
        band_tiles,
        tile_live.T,
        send_rows[0],
        recv_rows[0],
        edge_weight[0],
        live_slots,
        bias_terms.reshape(1, width),
        cotangent,
    )
    output, feature_grad, wg, bg = pl.pallas_call(
        finish,
        out_shape=tuple(jax.ShapeDtypeStruct(*r) for r in results),
        in_specs=[vmem] * 4,
        out_specs=(hbm,) * 4,
        scratch_shapes=[dma((4,))],
        compiler_params=pltpu.CompilerParams(vmem_limit_bytes=4 << 20),
    )(*parts)
    return (output, feature_grad, wg.T, bg.reshape(width))


def solution(mesh):
    return jax.shard_map(
        on_device,
        mesh=mesh,
        in_specs=(
            P(None, "dom"),
            P(None, "hid"),
            P(None, "dom"),
            P(None, "dom"),
            P("dom", None, None),
            P("dom", None, None),
            P("dom", None, None),
            P("dom", None),
            P("hid"),
            P("hid", "dom"),
        ),
        out_specs=(P("hid", "dom"), P("hid", "dom"), P(None, "hid"), P("hid")),
        check_vma=False,
    )
```
